512 devices in a mesh: dom: 64 (over y, z), grp: 8 (over x, core).
Axes of the slice: x: 4, y: 4, z: 16, core: 2. Of those that a mesh axis runs over, the one named last changes fastest.
Arguments:
- source: float32 [2048, 256, 128], P('dom', 'grp'), may hold values from -48 to 48
- conductivity: float32 [2048, 256, 128], P('dom', 'grp'), may hold values from 0.3 to 3
- absorption: float32 [2048, 256, 128], P('dom', 'grp'), may hold values from 0.1 to 2
- brick_mask: int32 [256, 32, 16], P('dom', 'grp'), may hold values 0 or 1
Outputs:
- fine_iterate: float32 [2048, 256, 128], P('dom', 'grp')
- fine_residual: float32 [2048, 256, 128], P('dom', 'grp')
- mid_iterate: float32 [1024, 128, 64], P('dom', 'grp')
- coarse_iterate: float32 [512, 64, 32], P('dom', 'grp')
The draws below stay inside these ranges and needn't reach their ends.
All inputs are finite; a program needn't handle non-finite values. No bound on the sum of `brick_mask` on one device may be relied on, other than what follows from the above.
Results may differ from the reference program's by a relative error of at most 0.00002.
Values sent between devices are 32-bit elements; how exact they have to be, the bound alone decides.
A program may use at most 192 MiB of HBM per device.

```python
import math
import jax
import jax.numpy as jnp

DEGREE = 4
COARSE_DEGREE = 6
NX = 2048
NY = 256
NZ = 128
NBX = 256
NBY = 32
NBZ = 16


def set_ends(drawn, own_key, smallest, high):
    index_at = [jax.random.randint(jax.random.fold_in(own_key, axis), (), 0, length) for axis, length in enumerate(drawn.shape)]
    widest = drawn.shape.index(max(drawn.shape))
    beside = index_at[:widest] + [(index_at[widest] + 1) % drawn.shape[widest]] + index_at[widest + 1:]
    return drawn.at[tuple(index_at)].set(smallest).at[tuple(beside)].set(high)


def steps_of(key, shape, cuts, least, top_value):
    level = 1.0
    for axis_at, shards_of in cuts:
        heights = jax.random.uniform(jax.random.fold_in(jax.random.fold_in(key, 6), axis_at), (shards_of,), jnp.float32, least / len(cuts), top_value / len(cuts))
        level = level * jnp.repeat(jnp.exp(heights), shape[axis_at] // shards_of).reshape((-1,) + (1,) * (len(shape) - 1 - axis_at))
    return level


def centred(key, extent, scale, limit, pieces=(), kind=jnp.bfloat16):
    factor_of = steps_of(key, extent, pieces, -0.22, 0.18) if pieces else 1.0
    values = jax.random.normal(key, extent, jnp.float32) * scale * factor_of
    return jnp.minimum(jnp.maximum(values, -limit), limit).astype(kind)


def setup_inputs(seed: int = 0) -> dict:
    splits = jax.random.split(jax.random.key(seed), 5)
    source = centred(splits[0], (NX, NY, NZ), 8.0, 48.0, ((0, 64), (1, 8)), jnp.float32)
    conductivity = jnp.clip(jnp.exp(math.log(3.0) - 2.3025851 * jax.random.uniform(splits[1], (NX, NY, NZ), jnp.float32) ** steps_of(splits[1], (NX, NY, NZ), ((0, 64), (1, 8)), -0.2, 0.2)), 0.3, 3.0)
    absorption = jnp.clip(jnp.exp(math.log(2.0) - 2.9957323 * jax.random.uniform(splits[2], (NX, NY, NZ), jnp.float32) ** steps_of(splits[2], (NX, NY, NZ), ((0, 64), (1, 8)), -0.2, 0.2)), 0.1, 2.0)
    brick_mask = set_ends((jax.random.randint(splits[3], (NBX, NBY, NBZ), 0, 4) < 3).astype(jnp.int32), jax.random.fold_in(splits[3], 1), 0, 1)
    return {"source": source, "conductivity": conductivity, "absorption": absorption, "brick_mask": brick_mask}


step_scale = 4.0
smooth_low = 0.3
smooth_high = 2.0
coarse_low = 0.05


def refine_mask(brick_flags):
    values = brick_flags.astype(jnp.float32)
    values = jnp.repeat(values, 8, axis=0)
    values = jnp.repeat(values, 8, axis=1)
    return jnp.repeat(values, 8, axis=2)


def six_views(padded):
    return [padded[2:, 1:-1, 1:-1], padded[:-2, 1:-1, 1:-1],
            padded[1:-1, 2:, 1:-1], padded[1:-1, :-2, 1:-1],
            padded[1:-1, 1:-1, 2:], padded[1:-1, 1:-1, :-2]]


def coefficients(kappa_pad, filled_pad, absorb_cells, factor):
    kappa_mid = kappa_pad[1:-1, 1:-1, 1:-1]
    weights = []
    summed = jnp.zeros_like(kappa_mid)
    counted = jnp.zeros_like(kappa_mid)
    for neighbour_kappa, neighbour_filled in zip(six_views(kappa_pad), six_views(filled_pad)):
        weight = factor * 0.5 * (kappa_mid + neighbour_kappa) * neighbour_filled
        weights.append(weight)
        summed = summed + weight
        counted = counted + neighbour_filled
    diagonal = 1.0 + summed + factor * absorb_cells * (6.0 - counted)
    return weights, diagonal


def apply_padded(field_pad, weights, diagonal, filled):
    center = field_pad[1:-1, 1:-1, 1:-1]
    neighbours = six_views(field_pad)
    coupled = weights[0] * neighbours[0]
    for index in range(1, 6):
        coupled = coupled + weights[index] * neighbours[index]
    return filled * (diagonal * center - coupled) + (1.0 - filled) * center


def chebyshev(source_term, diagonal, degree, lowest, highest, operate, keep_residual):
    middle = (highest + lowest) / 2.0
    spread = (highest - lowest) / 2.0
    relative = middle / spread
    factor_prev = 1.0 / relative
    inverse = 1.0 / diagonal
    update = (inverse * source_term) / middle
    iterate = update
    residual = source_term
    for sweep_index in range(degree):
        if sweep_index > 0:
            factor_next = 1.0 / (2.0 * relative - factor_prev)
            update = (factor_next * factor_prev) * update + (2.0 * factor_next / spread) * (inverse * residual)
            iterate = iterate + update
            factor_prev = factor_next
        if sweep_index < degree - 1 or keep_residual:
            residual = residual - operate(update)
    return iterate, residual


def coarsen(fields):
    shape_in = fields.shape
    blocks = fields.reshape(shape_in[0] // 2, 2, shape_in[1] // 2, 2, shape_in[2] // 2, 2)
    return jnp.mean(blocks, axis=(1, 3, 5))


def level_solve(source_term, kappa, absorb, filled, factor, degree, lowest, keep_residual):
    weights, diagonal = coefficients(jnp.pad(kappa, 1), jnp.pad(filled, 1), absorb, factor)

    def operate(vector):
        return apply_padded(jnp.pad(vector, 1), weights, diagonal, filled)

    return chebyshev(source_term, diagonal, degree, lowest, smooth_high, operate, keep_residual)


def reference(source, conductivity, absorption, brick_mask):
    filled = refine_mask(brick_mask)
    fine_iterate, fine_residual = level_solve(source * filled, conductivity, absorption, filled,
                                              step_scale, DEGREE, smooth_low, True)
    mid_kappa = coarsen(conductivity)
    mid_absorb = coarsen(absorption)
    mid_filled = coarsen(filled)
    mid_iterate, mid_residual = level_solve(coarsen(fine_residual), mid_kappa, mid_absorb, mid_filled,
                                            step_scale / 4.0, DEGREE, smooth_low, True)
    coarse_iterate = level_solve(coarsen(mid_residual), coarsen(mid_kappa), coarsen(mid_absorb),
                                 coarsen(mid_filled), step_scale / 16.0, COARSE_DEGREE, coarse_low, False)[0]
    return (fine_iterate, fine_residual, mid_iterate, coarse_iterate)
```

```python
import jax
import jax.numpy as jnp
from jax import lax
from jax.experimental import pallas as pl
from jax.experimental.pallas import tpu as pltpu
from jax.sharding import PartitionSpec as P

DEGREE = 4
COARSE_DEGREE = 6
STEP_SCALE = 4.0
SMOOTH_LOW = 0.3
SMOOTH_HIGH = 2.0
COARSE_LOW = 0.05
LANES = 128
MESH = pl.DeviceIdType.MESH
DIRS = tuple((a, b) for a in (-1, 0, 1) for b in (-1, 0, 1) if (a, b) != (0, 0))
F32 = jnp.float32


def recurrence(degree, lowest, highest):
    middle = (highest + lowest) / 2.0
    spread = (highest - lowest) / 2.0
    relative = middle / spread
    factor = 1.0 / relative
    steps = []
    for _ in range(degree - 1):
        following = 1.0 / (2.0 * relative - factor)
        steps.append((following * factor, 2.0 * following / spread))
        factor = following
    return 1.0 / middle, tuple(steps)


class Level:
    def __init__(self, n, margin, rows, stride, scale, degree, lowest):
        self.n, self.margin, self.stride, self.scale = n, margin, stride, scale
        self.nx = n + 2 * margin
        self.y0 = 8 - margin
        self.ny = rows
        self.yb = 8 * ((self.y0 + rows + 1 + 7) // 8)
        self.first, self.steps = recurrence(degree, lowest, SMOOTH_HIGH)
        self.degree = degree

    def coefficient_shape(self):
        return (self.n + 2 * self.margin + 2, self.yb, LANES)

    def source_shape(self):
        return (self.nx, self.yb, LANES)

    def work_shape(self):
        return (self.nx, self.ny + 16, LANES)


def span(sign, n, margin):
    if sign == 0:
        return 0, n
    return (n - margin, margin) if sign > 0 else (0, margin)


def landing(sign, n, margin, offset):
    if sign == 0:
        return offset
    return offset - margin if sign > 0 else offset + n


def lane_index():
    return lax.broadcasted_iota(jnp.int32, (1, LANES), 1)


def pool(read, write, count, stride):
    even = lax.rem(lane_index() // stride, 2) == 0

    def body(i, carry):
        p = (read(2 * i, 0) + read(2 * i, 1)) + (read(2 * i + 1, 0) + read(2 * i + 1, 1))
        other = jnp.where(even, pltpu.roll(p, LANES - stride, 1), pltpu.roll(p, stride, 1))
        write(i, (p + other) * 0.125)
        return carry

    lax.fori_loop(0, count, body, 0)


def setup(level, kappa, absorb, work):
    wx, wy, wz, diag, inv = work
    half = level.scale * 0.5
    up = lane_index() < LANES - level.stride
    down = lane_index() >= level.stride
    y0, ny = level.y0, level.ny

    def body(i, carry):
        k = kappa(i + 1, y0)
        xp, xm = kappa(i + 2, y0), kappa(i, y0)
        yp, ym = kappa(i + 1, y0 + 1), kappa(i + 1, y0 - 1)
        zp = jnp.where(up, pltpu.roll(k, LANES - level.stride, 1), 0.0)
        zm = jnp.where(down, pltpu.roll(k, level.stride, 1), 0.0)
        total = (xp + xm) + (yp + ym) + (zp + zm)
        count = jnp.zeros_like(k)
        for face in (xp, xm, yp, ym, zp, zm):
            count = count + jnp.where(face > 0.0, 1.0, 0.0)
        d = (1.0 + half * (k * count + total)) + level.scale * absorb(i, y0) * (6.0 - count)
        rows = pl.ds(8, ny)
        wx[i, rows, :] = half * (k + xp)
        wy[i, rows, :] = half * (k + yp)
        wz[i, rows, :] = jnp.where(up, half * (k + zp), 0.0)
        diag[i, rows, :] = d
        inv[i, rows, :] = jnp.where(k > 0.0, 1.0 / d, 0.0)
        return carry

    lax.fori_loop(0, level.nx, body, 0)


def start_iterate(level, source, inv, u0):
    rows = pl.ds(8, level.ny)

    def body(i, carry):
        u0[i, rows, :] = (inv[i, rows, :] * source(i, level.y0, level.ny)) * level.first
        return carry

    lax.fori_loop(0, level.nx, body, 0)


def residual_row(level, work, u, r, i, start, size):
    wx, wy, wz, diag, inv = work
    rows = pl.ds(start, size)
    c = u[i, rows, :]
    t = wx[i, rows, :] * u[i + 1, rows, :] + wx[i - 1, rows, :] * u[i - 1, rows, :]
    t = t + (wy[i, rows, :] * u[i, pl.ds(start + 1, size), :]
             + wy[i, pl.ds(start - 1, size), :] * u[i, pl.ds(start - 1, size), :])
    z = wz[i, rows, :]
    t = t + (z * pltpu.roll(c, LANES - level.stride, 1) + pltpu.roll(z * c, level.stride, 1))
    return (r - diag[i, rows, :] * c) + t, c


def sweeps(level, source, work, r, us, finish):
    inv = work[4]
    last = len(us) - 1
    m, n = level.margin, level.n
    for k in range(last):
        a, b = level.steps[k]

        def body(i, carry, k=k, a=a, b=b):
            rows = pl.ds(8, level.ny)
            old = source(i, level.y0, level.ny) if k == 0 else r[i, rows, :]
            new, c = residual_row(level, work, us[k], old, i, 8, level.ny)
            r[i, rows, :] = new
            us[k + 1][i, rows, :] = a * c + b * (inv[i, rows, :] * new)
            return carry

        lax.fori_loop(k + 1, level.nx - 1 - k, body, 0)

    own = 8 + m

    def body(i, carry):
        rows = pl.ds(own, n)
        new, c = residual_row(level, work, us[last], r[i, rows, :], i, own, n)
        total = us[0][i, rows, :]
        for u in us[1:-1]:
            total = total + u[i, rows, :]
        finish(i - m, new, total + c, c, inv[i, rows, :])
        return carry

    lax.fori_loop(m, m + n, body, 0)


def body_kernel(levels, s_in, k_in, a_in, b_in, it_out, res_out, mid_out, coarse_out,
                kf, sf, af, km, am, sm, kc, ac, sc, nb, bm, fm, midr, midi, coai,
                wf, wm, wc, rf, rm, rc, uf, um, uc, local, send, recv):
    fine, mid, coarse = levels
    d, g = lax.axis_index("dom"), lax.axis_index("grp")
    nd, ng = lax.axis_size("dom"), lax.axis_size("grp")

    loads = []
    for slot, (operand, buffer, off) in enumerate(
            ((k_in, kf, fine.margin + 1), (a_in, af, fine.margin), (s_in, sf, fine.margin))):
        copy = pltpu.make_async_copy(operand, buffer.at[pl.ds(off, fine.n), pl.ds(8, fine.n), :],
                                     local.at[slot])
        copy.start()
        loads.append(copy)

    def neighbour(dx, dg):
        return (lax.rem(d + (nd + dx), nd), lax.rem(g + (ng + dg), ng))

    barrier = pltpu.get_barrier_semaphore()
    for dx, dg in DIRS:
        pl.semaphore_signal(barrier, inc=1, device_id=neighbour(dx, dg), device_id_type=MESH)
    pl.semaphore_wait(barrier, len(DIRS))

    used = [0]

    def remote(src, dst, dx, dg):
        slot = used[0]
        used[0] += 1
        return pltpu.make_async_remote_copy(
            src_ref=src, dst_ref=dst, send_sem=send.at[slot], recv_sem=recv.at[slot],
            device_id=neighbour(dx, dg), device_id_type=MESH)

    def halo(src, dst, n, margin, offset, src_offset):
        copies = []
        for dx, dg in DIRS:
            sx, cx = span(dx, n, margin)
            sy, cy = span(dg, n, margin)
            ox, oy = src_offset
            copies.append(remote(
                src.at[pl.ds(sx + ox, cx), pl.ds(sy + oy, cy), :],
                dst.at[pl.ds(landing(dx, n, margin, offset), cx),
                       pl.ds(landing(dg, n, margin, 8), cy), :], dx, dg))
        for copy in copies:
            copy.start()
        return copies

    bricks = [remote(b_in, nb.at[slot], dx, dg) for slot, (dx, dg) in enumerate(DIRS)]
    for copy in bricks:
        copy.start()
    fine_k = halo(k_in, kf, fine.n, fine.margin + 1, fine.margin + 1, (0, 0))
    fine_a = halo(a_in, af, fine.n, fine.margin, fine.margin, (0, 0))
    fine_s = halo(s_in, sf, fine.n, fine.margin, fine.margin, (0, 0))

    lanes_of = (lax.broadcasted_iota(jnp.int32, (16, LANES), 1) // 8
                == lax.broadcasted_iota(jnp.int32, (16, LANES), 0)).astype(F32)
    bm[...] = jnp.zeros_like(bm)
    for bx in range(4):
        bm[pl.ds(8 * (1 + bx) + 1, 4), :] = b_in[bx].astype(F32)

    def spread_mask():
        fm[...] = jnp.dot(bm[...], lanes_of, preferred_element_type=F32)

    spread_mask()

    def mask_tile(x, row, t):
        flag = jnp.broadcast_to(fm[pl.ds(row + t, 1), :], (8, LANES))
        kf[x, pl.ds(8 * t, 8), :] = kf[x, pl.ds(8 * t, 8), :] * flag

    loads[0].wait()
    kx = fine.margin + 1

    def mask_own(x, carry):
        for t in range(1, 5):
            mask_tile(x + kx, 8 * (1 + x // 8), t)
        return carry

    lax.fori_loop(0, fine.n, mask_own, 0)
    loads[1].wait()
    loads[2].wait()

    def reader(ref, x0, count):
        return lambda x, y: ref[x + x0, pl.ds(8 + y, count, stride=2), :]

    def writer(ref, x0, count):
        def write(x, value):
            ref[x + x0, pl.ds(8, count), :] = value
        return write

    mx, cx = mid.margin + 1, coarse.margin + 1
    pool(reader(kf, kx, mid.n), writer(km, mx, mid.n), mid.n, fine.stride)
    pool(reader(af, fine.margin, mid.n), writer(am, mid.margin, mid.n), mid.n, fine.stride)
    pool(reader(km, mx, coarse.n), writer(kc, cx, coarse.n), coarse.n, mid.stride)
    pool(reader(am, mid.margin, coarse.n), writer(ac, coarse.margin, coarse.n), coarse.n, mid.stride)
    mid_k = halo(km, km, mid.n, mx, mx, (mx, 8))
    mid_a = halo(am, am, mid.n, mid.margin, mid.margin, (mid.margin, 8))
    coarse_k = halo(kc, kc, coarse.n, cx, cx, (cx, 8))
    coarse_a = halo(ac, ac, coarse.n, coarse.margin, coarse.margin, (coarse.margin, 8))

    inside = {-1: (d < nd - 1), 1: (d > 0), 0: None}
    inside_g = {-1: (g < ng - 1), 1: (g > 0), 0: None}
    keep_x = {s: 1.0 if v is None else v.astype(F32) for s, v in inside.items()}
    keep_y = {s: 1.0 if v is None else v.astype(F32) for s, v in inside_g.items()}
    for copy in bricks:
        copy.wait_recv()
    for slot, (dx, dg) in enumerate(DIRS):
        xs = {0: (0, 1, 2, 3), 1: (3,), -1: (0,)}[dx]
        ys, cy = {0: (0, 4), 1: (3, 1), -1: (0, 1)}[dg]
        for bx in xs:
            row = {0: 1 + bx, 1: 0, -1: 5}[dx]
            col = {0: 1, 1: 0, -1: 5}[dg]
            bm[pl.ds(8 * row + col, cy), :] = (
                nb[slot, bx, pl.ds(ys, cy), :].astype(F32) * (keep_x[dx] * keep_y[dg]))
    spread_mask()

    for copy in fine_k:
        copy.wait_recv()

    def mask_side(x, carry):
        for t in (0, 5):
            mask_tile(x + kx, 8 * (1 + x // 8), t)
        return carry

    lax.fori_loop(0, fine.n, mask_side, 0)

    def mask_ends(x, carry):
        for t in range(6):
            mask_tile(x, 0, t)
            mask_tile(x + kx + fine.n, 40, t)
        return carry

    lax.fori_loop(0, kx, mask_ends, 0)

    for copy in fine_a:
        copy.wait_recv()

    def at(ref, size):
        return lambda x, y: ref[x, pl.ds(y, size), :]

    def of(ref):
        return lambda x, y, size: ref[x, pl.ds(y, size), :]

    setup(fine, at(kf, fine.ny), at(af, fine.ny), wf)
    for copy in fine_s:
        copy.wait_recv()
    start_iterate(fine, of(sf), wf[4], uf[0])

    def fine_finish(x, new, total, c, inv):
        it_out[x] = total
        res_out[x] = jnp.where(inv > 0.0, new, 0.0)

    sweeps(fine, of(sf), wf, rf, uf, fine_finish)

    pool(lambda x, y: res_out[x, pl.ds(y, mid.n, stride=2), :], writer(sm, mid.margin, mid.n),
         mid.n, fine.stride)
    mid_s = halo(sm, sm, mid.n, mid.margin, mid.margin, (mid.margin, 8))

    def zero_outside(level, ref, copies):
        for copy in copies:
            copy.wait_recv()
        w = level.margin + 1

        def ends(x, carry):
            rows = pl.ds(0, level.yb)
            ref[x, rows, :] = ref[x, rows, :] * keep_x[1]
            ref[x + w + level.n, rows, :] = ref[x + w + level.n, rows, :] * keep_x[-1]
            return carry

        lax.fori_loop(0, w, ends, 0)

        def edges(x, carry):
            ref[x, pl.ds(0, 8), :] = ref[x, pl.ds(0, 8), :] * keep_y[1]
            high = pl.ds(8 + level.n, 8)
            ref[x, high, :] = ref[x, high, :] * keep_y[-1]
            return carry

        lax.fori_loop(0, level.n + 2 * w, edges, 0)

    zero_outside(mid, km, mid_k)
    for copy in mid_a:
        copy.wait_recv()
    setup(mid, at(km, mid.ny), at(am, mid.ny), wm)
    zero_outside(coarse, kc, coarse_k)
    for copy in coarse_a:
        copy.wait_recv()
    setup(coarse, at(kc, coarse.ny), at(ac, coarse.ny), wc)
    for copy in mid_s:
        copy.wait_recv()
    start_iterate(mid, of(sm), wm[4], um[0])

    def mid_finish(x, new, total, c, inv):
        midi[x] = total
        midr[x] = jnp.where(inv > 0.0, new, 0.0)

    sweeps(mid, of(sm), wm, rm, um, mid_finish)

    pool(lambda x, y: midr[x, pl.ds(y, coarse.n, stride=2), :],
         writer(sc, coarse.margin, coarse.n), coarse.n, mid.stride)
    coarse_s = halo(sc, sc, coarse.n, coarse.margin, coarse.margin, (coarse.margin, 8))

    def pick(value, stride):
        cells = LANES // stride
        chosen = (lax.broadcasted_iota(jnp.int32, (LANES, cells), 0)
                  == stride * lax.broadcasted_iota(jnp.int32, (LANES, cells), 1)).astype(F32)
        return jnp.dot(value, chosen, preferred_element_type=F32, precision=lax.Precision.HIGHEST)

    mid_out[...] = pick(midi[...].reshape(mid.n * mid.n, LANES), mid.stride).reshape(mid_out.shape)
    for copy in coarse_s:
        copy.wait_recv()
    start_iterate(coarse, of(sc), wc[4], uc[0])
    a, b = coarse.steps[-1]

    def coarse_finish(x, new, total, c, inv):
        coai[x] = total + (a * c + b * (inv * new))

    sweeps(coarse, of(sc), wc, rc, uc, coarse_finish)
    coarse_out[...] = pick(coai[...].reshape(coarse.n * coarse.n, LANES),
                           coarse.stride).reshape(coarse_out.shape)

    for group in (bricks, fine_k, fine_a, fine_s, mid_k, mid_a, coarse_k, coarse_a, mid_s, coarse_s):
        for copy in group:
            copy.wait_send()


def step(source, conductivity, absorption, brick_mask):
    n = source.shape[0]
    fine = Level(n, DEGREE, n + 2 * DEGREE, 1, STEP_SCALE, DEGREE, SMOOTH_LOW)
    mid = Level(n // 2, DEGREE, n // 2 + 2 * DEGREE, 2, STEP_SCALE / 4.0, DEGREE, SMOOTH_LOW)
    coarse = Level(n // 4, COARSE_DEGREE - 1, 24, 4, STEP_SCALE / 16.0, COARSE_DEGREE, COARSE_LOW)
    levels = (fine, mid, coarse)

    def kernel(*refs):
        body_kernel(levels, *refs)

    fields = []
    for level in levels:
        fields += [pltpu.VMEM(level.coefficient_shape(), F32), pltpu.VMEM(level.source_shape(), F32),
                   pltpu.VMEM(level.source_shape(), F32)]
    order = [fields[0], fields[1], fields[2], fields[3], fields[4], fields[5], fields[6], fields[7], fields[8]]
    copies = 10 * len(DIRS)
    scratch = order + [
        pltpu.VMEM((len(DIRS),) + brick_mask.shape, jnp.int32),
        pltpu.VMEM((48, 16), F32),
        pltpu.VMEM((48, LANES), F32),
        pltpu.VMEM((mid.n, mid.n, LANES), F32),
        pltpu.VMEM((mid.n, mid.n, LANES), F32),
        pltpu.VMEM((coarse.n, coarse.n, LANES), F32),
    ]
    scratch += [[pltpu.VMEM(level.work_shape(), F32)] * 5 for level in levels]
    scratch += [pltpu.VMEM(level.work_shape(), F32) for level in levels]
    scratch += [[pltpu.VMEM(level.work_shape(), F32)] * count
                for level, count in zip(levels, (DEGREE, DEGREE, COARSE_DEGREE - 1))]
    scratch += [pltpu.SemaphoreType.DMA((3,)), pltpu.SemaphoreType.DMA((copies,)),
                pltpu.SemaphoreType.DMA((copies,))]
    vmem = pl.BlockSpec(memory_space=pltpu.VMEM)
    anywhere = pl.BlockSpec(memory_space=pl.ANY)
    return pl.pallas_call(
        kernel,
        out_shape=(
            jax.ShapeDtypeStruct((n, n, LANES), F32),
            jax.ShapeDtypeStruct((n, n, LANES), F32),
            jax.ShapeDtypeStruct((mid.n, mid.n, LANES // 2), F32),
            jax.ShapeDtypeStruct((coarse.n, coarse.n, LANES // 4), F32),
        ),
        in_specs=[anywhere, anywhere, anywhere, vmem],
        out_specs=(vmem, vmem, vmem, vmem),
        scratch_shapes=scratch,
        compiler_params=pltpu.CompilerParams(collective_id=0, has_side_effects=True,
                                             vmem_limit_bytes=56 * 1024 * 1024),
    )(source, conductivity, absorption, brick_mask)


def solution(mesh):
    spec = P("dom", "grp", None)
    return jax.shard_map(step, mesh=mesh, in_specs=(spec,) * 4, out_specs=(spec,) * 4, check_vma=False)
```

```python
import jax
import jax.numpy as jnp
from jax import lax
from jax.experimental import pallas as pl
from jax.experimental.pallas import tpu as pltpu
from jax.sharding import PartitionSpec as P

DEGREE = 4
COARSE_DEGREE = 6
STEP_SCALE = 4.0
SMOOTH_LOW = 0.3
SMOOTH_HIGH = 2.0
COARSE_LOW = 0.05
LANES = 128
MESH = pl.DeviceIdType.MESH
DIRS = ((1, 0), (1, 1), (1, -1), (0, 1), (0, -1), (-1, 0), (-1, 1), (-1, -1))
BLOCK = 4
F32 = jnp.float32


def recurrence(degree, lowest, highest):
    middle = (highest + lowest) / 2.0
    spread = (highest - lowest) / 2.0
    relative = middle / spread
    factor = 1.0 / relative
    steps = []
    for _ in range(degree - 1):
        following = 1.0 / (2.0 * relative - factor)
        steps.append((following * factor, 2.0 * following / spread))
        factor = following
    return 1.0 / middle, tuple(steps)


class Level:
    def __init__(self, n, margin, rows, stride, scale, degree, lowest):
        self.n, self.margin, self.stride, self.scale = n, margin, stride, scale
        self.nx = n + 2 * margin
        self.y0 = 8 - margin
        self.ny = rows
        self.yb = 8 * ((self.y0 + rows + 1 + 7) // 8)
        self.first, self.steps = recurrence(degree, lowest, SMOOTH_HIGH)
        self.degree = degree

    def coefficient_shape(self):
        return (self.n + 2 * self.margin + 2, self.yb, LANES)

    def source_shape(self):
        return (self.nx, self.yb, LANES)

    def work_shape(self):
        return (self.nx, self.ny + 16, LANES)


def span(sign, n, margin):
    if sign == 0:
        return 0, n
    return (n - margin, margin) if sign > 0 else (0, margin)


def landing(sign, n, margin, offset):
    if sign == 0:
        return offset
    return offset - margin if sign > 0 else offset + n


def lane_index():
    return lax.broadcasted_iota(jnp.int32, (1, LANES), 1)


def blocks(low, high, body):
    steps, rest = divmod(high - low, BLOCK)

    def turn(s, carry):
        body(low + s * BLOCK, BLOCK)
        return carry

    if steps:
        lax.fori_loop(0, steps, turn, 0)
    if rest:
        body(high - rest, rest)


def pool(read, write, count, stride):
    even = lax.rem(lane_index() // stride, 2) == 0

    def body(first, rows):
        for i in range(rows):
            x = 2 * (first + i)
            p = (read(x, 0) + read(x, 1)) + (read(x + 1, 0) + read(x + 1, 1))
            other = jnp.where(even, pltpu.roll(p, LANES - stride, 1), pltpu.roll(p, stride, 1))
            write(first + i, (p + other) * 0.125)

    blocks(0, count, body)


def setup(level, kappa, absorb, work, source=None, u0=None):
    wx, wy, wz, diag, inv = work
    half = level.scale * 0.5
    up = lane_index() < LANES - level.stride
    down = lane_index() >= level.stride
    y0, ny = level.y0, level.ny

    def flag(k):
        return jnp.where(k > 0.0, 1.0, 0.0)

    def body(first, rows):
        ks = [kappa(first + x, y0) for x in range(rows + 2)]
        flags = [flag(k) for k in ks]
        for r in range(rows):
            i = first + r
            k, xp, xm = ks[r + 1], ks[r + 2], ks[r]
            yp, ym = kappa(i + 1, y0 + 1), kappa(i + 1, y0 - 1)
            zp = jnp.where(up, pltpu.roll(k, LANES - level.stride, 1), 0.0)
            zm = jnp.where(down, pltpu.roll(k, level.stride, 1), 0.0)
            total = (xp + xm) + (yp + ym) + (zp + zm)
            count = (flags[r + 2] + flags[r]) + (flag(yp) + flag(ym)) + (flag(zp) + flag(zm))
            d = (1.0 + half * (k * count + total)) + level.scale * absorb(i, y0) * (6.0 - count)
            at = pl.ds(8, ny)
            wx[i, at, :] = half * (k + xp)
            wy[i, at, :] = half * (k + yp)
            wz[i, at, :] = jnp.where(up, half * (k + zp), 0.0)
            diag[i, at, :] = d
            v = flags[r + 1] / d
            inv[i, at, :] = v
            if u0 is not None:
                u0[i, at, :] = (v * source(i, y0, ny)) * level.first

    blocks(0, level.nx, body)


def start_iterate(level, source, inv, u0):
    at = pl.ds(8, level.ny)

    def body(first, rows):
        for i in range(rows):
            u0[first + i, at, :] = (inv[first + i, at, :] * source(first + i, level.y0, level.ny)) * level.first

    blocks(0, level.nx, body)


def residual_rows(level, work, u, old, first, rows, start, size):
    wx, wy, wz, diag, inv = work
    at, above, below = pl.ds(start, size), pl.ds(start + 1, size), pl.ds(start - 1, size)
    us = [u[first + x - 1, at, :] for x in range(rows + 2)]
    ws = [wx[first + x - 1, at, :] for x in range(rows + 1)]
    out = []
    for r in range(rows):
        i, c = first + r, us[r + 1]
        t = ws[r + 1] * us[r + 2] + ws[r] * us[r]
        t = t + (wy[i, at, :] * u[i, above, :] + wy[i, below, :] * u[i, below, :])
        z = wz[i, at, :]
        t = t + (z * pltpu.roll(c, LANES - level.stride, 1) + pltpu.roll(z * c, level.stride, 1))
        out.append(((old(i) - diag[i, at, :] * c) + t, c))
    return out


def sweeps(level, source, work, r, us, finish):
    inv = work[4]
    last = len(us) - 1
    m, n = level.margin, level.n
    at = pl.ds(8, level.ny)
    for k in range(last):
        a, b = level.steps[k]

        def body(first, rows, k=k, a=a, b=b):
            def old(i):
                return source(i, level.y0, level.ny) if k == 0 else r[i, at, :]

            for x, (new, c) in enumerate(
                    residual_rows(level, work, us[k], old, first, rows, 8, level.ny)):
                r[first + x, at, :] = new
                us[k + 1][first + x, at, :] = a * c + b * (inv[first + x, at, :] * new)

        blocks(k + 1, level.nx - 1 - k, body)

    own = pl.ds(8 + m, n)

    def body(first, rows):
        for x, (new, c) in enumerate(
                residual_rows(level, work, us[last], lambda i: r[i, own, :], first, rows, 8 + m, n)):
            total = us[0][first + x, own, :]
            for u in us[1:-1]:
                total = total + u[first + x, own, :]
            finish(first + x - m, new, total + c, c, inv[first + x, own, :])

    blocks(m, m + n, body)


def body_kernel(levels, s_in, k_in, a_in, b_in, it_out, res_out, mid_out, coarse_out,
                kf, sf, af, km, am, sm, kc, ac, sc, fm, midr, midi, coai,
                wf, wm, wc, rf, rm, rc, uf, um, uc, local, send, recv):
    fine, mid, coarse = levels
    d, g = lax.axis_index("dom"), lax.axis_index("grp")
    nd, ng = lax.axis_size("dom"), lax.axis_size("grp")
    low_x, high_x = d > 0, d < nd - 1
    low_y, high_y = g > 0, g < ng - 1

    def both(p, q):
        return q if p is None else p if q is None else jnp.logical_and(p, q)

    def target(dx, dg):
        return both({0: None, 1: high_x, -1: low_x}[dx], {0: None, 1: high_y, -1: low_y}[dg])

    def neighbour(dx, dg):
        return (lax.rem(d + (nd + dx), nd), lax.rem(g + (ng + dg), ng))

    barrier = pltpu.get_barrier_semaphore()
    for dx, dg in DIRS:
        @pl.when(target(dx, dg))
        def _(dx=dx, dg=dg):
            pl.semaphore_signal(barrier, inc=1, device_id=neighbour(dx, dg), device_id_type=MESH)

    loads = []
    for slot, (operand, buffer, off) in enumerate(
            ((k_in, kf, fine.margin + 1), (a_in, af, fine.margin), (s_in, sf, fine.margin))):
        copy = pltpu.make_async_copy(operand, buffer.at[pl.ds(off, fine.n), pl.ds(8, fine.n), :],
                                     local.at[slot])
        copy.start()
        loads.append(copy)

    fields = ((kf, fine, 1), (af, fine, 0), (sf, fine, 0), (km, mid, 1), (am, mid, 0), (sm, mid, 0),
              (kc, coarse, 1), (ac, coarse, 0), (sc, coarse, 0))
    for ref, level, extra in fields:
        w = level.margin + extra
        rows, cells = level.n + 2 * w, level.n
        for missing, x0 in ((d == 0, 0), (d == nd - 1, w + cells)):
            @pl.when(missing)
            def _(ref=ref, level=level, w=w, x0=x0):
                for x in range(w):
                    ref[x0 + x] = jnp.zeros((level.yb, LANES), F32)
        for missing, y0 in ((g == 0, 0), (g == ng - 1, 8 + cells)):
            @pl.when(missing)
            def _(ref=ref, rows=rows, y0=y0):
                def clear(x, carry):
                    ref[x, pl.ds(y0, 8), :] = jnp.zeros((8, LANES), F32)
                    return carry
                lax.fori_loop(0, rows, clear, 0)

    lanes_of = (lax.broadcasted_iota(jnp.int32, (16, LANES), 1) // 8
                == lax.broadcasted_iota(jnp.int32, (16, LANES), 0)).astype(F32)
    for bx in range(4):
        fm[pl.ds(8 * bx, 4), :] = jnp.dot(b_in[bx].astype(F32), lanes_of, preferred_element_type=F32)

    loads[0].wait()
    kx = fine.margin + 1

    def mask_own(s, carry):
        for t in range(4):
            flag = jnp.broadcast_to(fm[pl.ds(8 * (s // 2) + t, 1), :], (8, LANES))
            for x in range(4):
                at = (kx + 4 * s + x, pl.ds(8 + 8 * t, 8), slice(None))
                kf[at] = kf[at] * flag
        return carry

    lax.fori_loop(0, fine.n // 4, mask_own, 0)
    loads[1].wait()
    loads[2].wait()
    count_x = low_x.astype(jnp.int32) + high_x.astype(jnp.int32) + 1
    count_y = low_y.astype(jnp.int32) + high_y.astype(jnp.int32) + 1
    pl.semaphore_wait(barrier, count_x * count_y - 1)

    used = [0]
    groups = []

    def halo(parts):
        group = []
        for dx, dg in DIRS:
            copies = []
            for ref, level, width in parts:
                n = level.n
                sx, cx = span(dx, n, width)
                sy, cy = span(dg, n, width)
                slot = used[0]
                used[0] += 1
                copies.append(pltpu.make_async_remote_copy(
                    src_ref=ref.at[pl.ds(width + sx, cx), pl.ds(8 + sy, cy), :],
                    dst_ref=ref.at[pl.ds(landing(dx, n, width, width), cx),
                                   pl.ds(landing(dg, n, width, 8), cy), :],
                    send_sem=send.at[slot], recv_sem=recv.at[slot],
                    device_id=neighbour(dx, dg), device_id_type=MESH))

            @pl.when(target(dx, dg))
            def _(copies=copies):
                for copy in copies:
                    copy.start()

            group.append((dx, dg, copies))
        groups.append(group)
        return group

    def arrive(group):
        for dx, dg, copies in group:
            @pl.when(target(-dx, -dg))
            def _(copies=copies):
                for copy in copies:
                    copy.wait_recv()

    mx, cx = mid.margin + 1, coarse.margin + 1
    fine_halo = halo(((kf, fine, kx), (af, fine, fine.margin), (sf, fine, fine.margin)))

    def reader(ref, x0, count):
        return lambda x, y: ref[x + x0, pl.ds(8 + y, count, stride=2), :]

    def writer(ref, x0, count):
        def write(x, value):
            ref[x + x0, pl.ds(8, count), :] = value
        return write

    pool(reader(kf, kx, mid.n), writer(km, mx, mid.n), mid.n, fine.stride)
    pool(reader(af, fine.margin, mid.n), writer(am, mid.margin, mid.n), mid.n, fine.stride)
    pool(reader(km, mx, coarse.n), writer(kc, cx, coarse.n), coarse.n, mid.stride)
    pool(reader(am, mid.margin, coarse.n), writer(ac, coarse.margin, coarse.n), coarse.n, mid.stride)
    side_halo = halo(((km, mid, mx), (am, mid, mid.margin), (kc, coarse, cx), (ac, coarse, coarse.margin)))

    def at(ref, size):
        return lambda x, y: ref[x, pl.ds(y, size), :]

    def of(ref):
        return lambda x, y, size: ref[x, pl.ds(y, size), :]

    arrive(fine_halo)
    setup(fine, at(kf, fine.ny), at(af, fine.ny), wf, of(sf), uf[0])

    def fine_finish(x, new, total, c, inv):
        it_out[x] = total
        res_out[x] = jnp.where(inv > 0.0, new, 0.0)

    sweeps(fine, of(sf), wf, rf, uf, fine_finish)

    pool(lambda x, y: res_out[x, pl.ds(y, mid.n, stride=2), :], writer(sm, mid.margin, mid.n),
         mid.n, fine.stride)
    mid_halo = halo(((sm, mid, mid.margin),))
    arrive(side_halo)
    setup(mid, at(km, mid.ny), at(am, mid.ny), wm)
    setup(coarse, at(kc, coarse.ny), at(ac, coarse.ny), wc)
    arrive(mid_halo)
    start_iterate(mid, of(sm), wm[4], um[0])

    def mid_finish(x, new, total, c, inv):
        midi[x] = total
        midr[x] = jnp.where(inv > 0.0, new, 0.0)

    sweeps(mid, of(sm), wm, rm, um, mid_finish)

    pool(lambda x, y: midr[x, pl.ds(y, coarse.n, stride=2), :],
         writer(sc, coarse.margin, coarse.n), coarse.n, mid.stride)
    coarse_halo = halo(((sc, coarse, coarse.margin),))

    def pick(value, stride):
        cells = LANES // stride
        chosen = (lax.broadcasted_iota(jnp.int32, (LANES, cells), 0)
                  == stride * lax.broadcasted_iota(jnp.int32, (LANES, cells), 1)).astype(F32)
        return jnp.dot(value, chosen, preferred_element_type=F32, precision=lax.Precision.HIGHEST)

    mid_out[...] = pick(midi[...].reshape(mid.n * mid.n, LANES), mid.stride).reshape(mid_out.shape)
    arrive(coarse_halo)
    start_iterate(coarse, of(sc), wc[4], uc[0])
    a, b = coarse.steps[-1]

    def coarse_finish(x, new, total, c, inv):
        coai[x] = total + (a * c + b * (inv * new))

    sweeps(coarse, of(sc), wc, rc, uc, coarse_finish)
    coarse_out[...] = pick(coai[...].reshape(coarse.n * coarse.n, LANES),
                           coarse.stride).reshape(coarse_out.shape)

    for position in range(len(DIRS)):
        dx, dg = DIRS[position]

        @pl.when(target(dx, dg))
        def _(position=position):
            for group in groups:
                for copy in group[position][2]:
                    copy.wait_send()


def step(source, conductivity, absorption, brick_mask):
    n = source.shape[0]
    fine = Level(n, DEGREE, n + 2 * DEGREE, 1, STEP_SCALE, DEGREE, SMOOTH_LOW)
    mid = Level(n // 2, DEGREE, n // 2 + 2 * DEGREE, 2, STEP_SCALE / 4.0, DEGREE, SMOOTH_LOW)
    coarse = Level(n // 4, COARSE_DEGREE - 1, 24, 4, STEP_SCALE / 16.0, COARSE_DEGREE, COARSE_LOW)
    levels = (fine, mid, coarse)

    def kernel(*refs):
        body_kernel(levels, *refs)

    fields = []
    for level in levels:
        fields += [pltpu.VMEM(level.coefficient_shape(), F32), pltpu.VMEM(level.source_shape(), F32),
                   pltpu.VMEM(level.source_shape(), F32)]
    copies = 9 * len(DIRS)
    scratch = fields + [
        pltpu.VMEM((32, LANES), F32),
        pltpu.VMEM((mid.n, mid.n, LANES), F32),
        pltpu.VMEM((mid.n, mid.n, LANES), F32),
        pltpu.VMEM((coarse.n, coarse.n, LANES), F32),
    ]
    scratch += [[pltpu.VMEM(level.work_shape(), F32)] * 5 for level in levels]
    scratch += [pltpu.VMEM(level.work_shape(), F32) for level in levels]
    scratch += [[pltpu.VMEM(level.work_shape(), F32)] * count
                for level, count in zip(levels, (DEGREE, DEGREE, COARSE_DEGREE - 1))]
    scratch += [pltpu.SemaphoreType.DMA((3,)), pltpu.SemaphoreType.DMA((copies,)),
                pltpu.SemaphoreType.DMA((copies,))]
    vmem = pl.BlockSpec(memory_space=pltpu.VMEM)
    anywhere = pl.BlockSpec(memory_space=pl.ANY)
    return pl.pallas_call(
        kernel,
        out_shape=(
            jax.ShapeDtypeStruct((n, n, LANES), F32),
            jax.ShapeDtypeStruct((n, n, LANES), F32),
            jax.ShapeDtypeStruct((mid.n, mid.n, LANES // 2), F32),
            jax.ShapeDtypeStruct((coarse.n, coarse.n, LANES // 4), F32),
        ),
        in_specs=[anywhere, anywhere, anywhere, vmem],
        out_specs=(vmem, vmem, vmem, vmem),
        scratch_shapes=scratch,
        compiler_params=pltpu.CompilerParams(collective_id=0, has_side_effects=True,
                                             vmem_limit_bytes=56 * 1024 * 1024),
    )(source, conductivity, absorption, brick_mask)


def solution(mesh):
    spec = P("dom", "grp", None)
    return jax.shard_map(step, mesh=mesh, in_specs=(spec,) * 4, out_specs=(spec,) * 4, check_vma=False)
```

```python
import jax
import jax.numpy as jnp
from jax import lax
from jax.experimental import pallas as pl
from jax.experimental.pallas import tpu as pltpu
from jax.sharding import PartitionSpec as P

DEGREE = 4
COARSE_DEGREE = 6
STEP_SCALE = 4.0
SMOOTH_LOW = 0.3
SMOOTH_HIGH = 2.0
COARSE_LOW = 0.05
LANES = 128
MESH = pl.DeviceIdType.MESH
DIRS = ((0, 1), (0, -1), (1, 0), (1, 1), (1, -1), (-1, 0), (-1, 1), (-1, -1))
BLOCK = 14
FAR_FIRST = ((1, 1), (1, -1), (-1, 1), (-1, -1), (1, 0), (-1, 0), (0, 1), (0, -1))
F32 = jnp.float32


def recurrence(degree, lowest, highest):
    middle = (highest + lowest) / 2.0
    spread = (highest - lowest) / 2.0
    relative = middle / spread
    factor = 1.0 / relative
    steps = []
    for _ in range(degree - 1):
        following = 1.0 / (2.0 * relative - factor)
        steps.append((following * factor, 2.0 * following / spread))
        factor = following
    return 1.0 / middle, tuple(steps)


class Level:
    def __init__(self, n, margin, rows, stride, scale, degree, lowest):
        self.n, self.margin, self.stride, self.scale = n, margin, stride, scale
        self.nx = n + 2 * margin
        self.y0 = 8 - margin
        self.ny = rows
        self.yb = 8 * ((self.y0 + rows + 1 + 7) // 8)
        self.first, self.steps = recurrence(degree, lowest, SMOOTH_HIGH)
        self.block = BLOCK if rows > 24 else 24

    def coefficient_shape(self):
        return (self.n + 2 * self.margin + 2, self.yb, LANES)

    def source_shape(self):
        return (self.nx, self.yb, LANES)

    def work_shape(self):
        return (self.nx, self.ny + 16, LANES)


def span(sign, n, margin):
    if sign == 0:
        return 0, n
    return (n - margin, margin) if sign > 0 else (0, margin)


def landing(sign, n, margin, offset):
    if sign == 0:
        return offset
    return offset - margin if sign > 0 else offset + n


def lane_index():
    return lax.broadcasted_iota(jnp.int32, (1, LANES), 1)


def blocks(low, high, body, most=BLOCK):
    steps, rest = divmod(high - low, most)

    def turn(s, carry):
        body(low + s * most, most)
        return carry

    if steps == 1:
        body(low, most)
    elif steps:
        lax.fori_loop(0, steps, turn, 0)
    if rest:
        body(high - rest, rest)


def pool(read, write, count, stride):
    even = lax.rem(lane_index() // stride, 2) == 0

    def body(first, rows):
        for i in range(rows):
            x = 2 * (first + i)
            p = (read(x, 0) + read(x, 1)) + (read(x + 1, 0) + read(x + 1, 1))
            other = jnp.where(even, pltpu.roll(p, LANES - stride, 1), pltpu.roll(p, stride, 1))
            write(first + i, (p + other) * 0.125)

    blocks(0, count, body)


def setup(level, kappa, absorb, work, source=None, u0=None, span_x=None):
    wx, wy, wz, diag, inv = work
    half = level.scale * 0.5
    up = lane_index() < LANES - level.stride
    down = lane_index() >= level.stride
    y0, ny = level.y0, level.ny

    def flag(k):
        return jnp.where(k > 0.0, 1.0, 0.0)

    def body(first, rows):
        ks = [kappa(first + x, y0) for x in range(rows + 2)]
        flags = [flag(k) for k in ks]
        for r in range(rows):
            i = first + r
            k, xp, xm = ks[r + 1], ks[r + 2], ks[r]
            yp, ym = kappa(i + 1, y0 + 1), kappa(i + 1, y0 - 1)
            zp = jnp.where(up, pltpu.roll(k, LANES - level.stride, 1), 0.0)
            zm = jnp.where(down, pltpu.roll(k, level.stride, 1), 0.0)
            total = (xp + xm) + (yp + ym) + (zp + zm)
            count = (flags[r + 2] + flags[r]) + (flag(yp) + flag(ym)) + (flag(zp) + flag(zm))
            d = (1.0 + half * (k * count + total)) + level.scale * absorb(i, y0) * (6.0 - count)
            at = pl.ds(8, ny)
            wx[i, at, :] = half * (k + xp)
            wy[i, at, :] = half * (k + yp)
            wz[i, at, :] = jnp.where(up, half * (k + zp), 0.0)
            diag[i, at, :] = d
            v = flags[r + 1] / d
            inv[i, at, :] = v
            if u0 is not None:
                u0[i, at, :] = (v * source(i, y0, ny)) * level.first

    blocks(*(span_x or (0, level.nx)), body, level.block)


def start_iterate(level, source, inv, u0):
    at = pl.ds(8, level.ny)

    def body(first, rows):
        for i in range(rows):
            u0[first + i, at, :] = (inv[first + i, at, :] * source(first + i, level.y0, level.ny)) * level.first

    blocks(0, level.nx, body, level.block)


def residual_rows(level, work, u, old, first, rows, start, size):
    wx, wy, wz, diag, inv = work
    at, above, below = pl.ds(start, size), pl.ds(start + 1, size), pl.ds(start - 1, size)
    us = [u[first + x - 1, at, :] for x in range(rows + 2)]
    ws = [wx[first + x - 1, at, :] for x in range(rows + 1)]
    out = []
    for r in range(rows):
        i, c = first + r, us[r + 1]
        t = ws[r + 1] * us[r + 2] + ws[r] * us[r]
        t = t + (wy[i, at, :] * u[i, above, :] + wy[i, below, :] * u[i, below, :])
        z = wz[i, at, :]
        t = t + (z * pltpu.roll(c, LANES - level.stride, 1) + pltpu.roll(z * c, level.stride, 1))
        out.append(((old(i) - diag[i, at, :] * c) + t, c))
    return out


def sweeps(level, source, work, r, us, finish, span_of=None):
    inv = work[4]
    last = len(us) - 1
    m, n = level.margin, level.n
    at = pl.ds(8, level.ny)
    span_of = span_of or (lambda k: (k + 1, level.nx - 1 - k))
    for k in range(last):
        a, b = level.steps[k]

        def body(first, rows, k=k, a=a, b=b):
            def old(i):
                return source(i, level.y0, level.ny) if k == 0 else r[i, at, :]

            for x, (new, c) in enumerate(
                    residual_rows(level, work, us[k], old, first, rows, 8, level.ny)):
                r[first + x, at, :] = new
                us[k + 1][first + x, at, :] = a * c + b * (inv[first + x, at, :] * new)

        blocks(*span_of(k), body, level.block)

    own = pl.ds(8 + m, n)

    def body(first, rows):
        for x, (new, c) in enumerate(
                residual_rows(level, work, us[last], lambda i: r[i, own, :], first, rows, 8 + m, n)):
            total = us[0][first + x, own, :]
            for u in us[1:-1]:
                total = total + u[first + x, own, :]
            finish(first + x - m, new, total + c, c, inv[first + x, own, :])

    blocks(*span_of(last), body, level.block)


def body_kernel(levels, s_in, k_in, a_in, b_in, it_out, res_out, mid_out, coarse_out,
                kf, sf, af, km, am, sm, kc, ac, sc, fm, midr, midi, coai,
                wf, wm, wc, rf, rm, rc, uf, um, uc, local, send, recv):
    fine, mid, coarse = levels
    d, g = lax.axis_index("dom"), lax.axis_index("grp")
    nd, ng = lax.axis_size("dom"), lax.axis_size("grp")
    low_x, high_x = d > 0, d < nd - 1
    low_y, high_y = g > 0, g < ng - 1

    def both(p, q):
        return q if p is None else p if q is None else jnp.logical_and(p, q)

    def target(dx, dg):
        return both({0: None, 1: high_x, -1: low_x}[dx], {0: None, 1: high_y, -1: low_y}[dg])

    def neighbour(dx, dg):
        return (lax.rem(d + (nd + dx), nd), lax.rem(g + (ng + dg), ng))

    barrier = pltpu.get_barrier_semaphore()
    for dx, dg in DIRS:
        @pl.when(target(dx, dg))
        def _(dx=dx, dg=dg):
            pl.semaphore_signal(barrier, inc=1, device_id=neighbour(dx, dg), device_id_type=MESH)

    loads = []
    for slot, (operand, buffer, off) in enumerate(
            ((k_in, kf, fine.margin + 1), (a_in, af, fine.margin), (s_in, sf, fine.margin))):
        copy = pltpu.make_async_copy(operand, buffer.at[pl.ds(off, fine.n), pl.ds(8, fine.n), :],
                                     local.at[slot])
        copy.start()
        loads.append(copy)

    fields = ((kf, fine, 1), (af, fine, 0), (sf, fine, 0), (km, mid, 1), (am, mid, 0), (sm, mid, 0),
              (kc, coarse, 1), (ac, coarse, 0), (sc, coarse, 0))
    for ref, level, extra in fields:
        w = level.margin + extra
        rows, cells = level.n + 2 * w, level.n
        for missing, x0 in ((d == 0, 0), (d == nd - 1, w + cells)):
            @pl.when(missing)
            def _(ref=ref, level=level, w=w, x0=x0):
                for x in range(w):
                    ref[x0 + x] = jnp.zeros((level.yb, LANES), F32)
        for missing, y0 in ((g == 0, 0), (g == ng - 1, 8 + cells)):
            @pl.when(missing)
            def _(ref=ref, rows=rows, y0=y0):
                def clear(x, carry):
                    ref[x, pl.ds(y0, 8), :] = jnp.zeros((8, LANES), F32)
                    return carry
                lax.fori_loop(0, rows, clear, 0)

    lanes_of = (lax.broadcasted_iota(jnp.int32, (16, LANES), 1) // 8
                == lax.broadcasted_iota(jnp.int32, (16, LANES), 0)).astype(F32)
    for bx in range(4):
        fm[pl.ds(8 * bx, 4), :] = jnp.dot(b_in[bx].astype(F32), lanes_of, preferred_element_type=F32)

    count_x = low_x.astype(jnp.int32) + high_x.astype(jnp.int32) + 1
    count_y = low_y.astype(jnp.int32) + high_y.astype(jnp.int32) + 1

    loads[0].wait()
    kx = fine.margin + 1

    def mask_own(s, carry):
        for t in range(4):
            flag = jnp.broadcast_to(fm[pl.ds(8 * (s // 2) + t, 1), :], (8, LANES))
            for x in range(4):
                at = (kx + 4 * s + x, pl.ds(8 + 8 * t, 8), slice(None))
                kf[at] = kf[at] * flag
        return carry

    lax.fori_loop(0, fine.n // 4, mask_own, 0)
    loads[1].wait()
    loads[2].wait()

    pl.semaphore_wait(barrier, count_x * count_y - 1)

    used = [0]
    groups = []

    def halo(parts, order):
        group = {}
        for dx, dg in order:
            copies = []
            for ref, level, width in parts:
                n = level.n
                sx, cx = span(dx, n, width)
                sy, cy = span(dg, n, width)
                slot = used[0]
                used[0] += 1
                copies.append(pltpu.make_async_remote_copy(
                    src_ref=ref.at[pl.ds(width + sx, cx), pl.ds(8 + sy, cy), :],
                    dst_ref=ref.at[pl.ds(landing(dx, n, width, width), cx),
                                   pl.ds(landing(dg, n, width, 8), cy), :],
                    send_sem=send.at[slot], recv_sem=recv.at[slot],
                    device_id=neighbour(dx, dg), device_id_type=MESH))

            @pl.when(target(dx, dg))
            def _(copies=copies):
                for copy in copies:
                    copy.start()

            group[dx, dg] = copies
        groups.append(group)
        return group

    def arrive(group, signs=(-1, 0, 1)):
        for (dx, dg), copies in group.items():
            if dx not in signs:
                continue

            @pl.when(target(-dx, -dg))
            def _(copies=copies):
                for copy in copies:
                    copy.wait_recv()

    mx, cx = mid.margin + 1, coarse.margin + 1
    fine_halo = halo(((kf, fine, kx), (af, fine, fine.margin), (sf, fine, fine.margin)), DIRS)

    def reader(ref, x0, count):
        return lambda x, y: ref[x + x0, pl.ds(8 + y, count, stride=2), :]

    def writer(ref, x0, count):
        def write(x, value):
            ref[x + x0, pl.ds(8, count), :] = value
        return write

    pool(reader(kf, kx, mid.n), writer(km, mx, mid.n), mid.n, fine.stride)
    pool(reader(af, fine.margin, mid.n), writer(am, mid.margin, mid.n), mid.n, fine.stride)
    pool(reader(km, mx, coarse.n), writer(kc, cx, coarse.n), coarse.n, mid.stride)
    pool(reader(am, mid.margin, coarse.n), writer(ac, coarse.margin, coarse.n), coarse.n, mid.stride)
    side_halo = halo(((km, mid, mx), (am, mid, mid.margin), (kc, coarse, cx), (ac, coarse, coarse.margin)),
                     DIRS)

    def at(ref, size):
        return lambda x, y: ref[x, pl.ds(y, size), :]

    def of(ref):
        return lambda x, y, size: ref[x, pl.ds(y, size), :]

    def fine_finish(x, new, total, c, inv):
        it_out[x] = total
        res_out[x] = jnp.where(inv > 0.0, new, 0.0)

    def fine_part(low, high, span_of):
        setup(fine, at(kf, fine.ny), at(af, fine.ny), wf, of(sf), uf[0], (low, high))
        sweeps(fine, of(sf), wf, rf, uf, fine_finish, span_of)

    edge, end = fine.margin + 1, fine.nx - fine.margin - 1
    arrive(fine_halo, (0,))
    fine_part(edge, end, lambda k: (edge + 1 + k, end - 1 - k))
    arrive(fine_halo, (-1,))
    fine_part(end, fine.nx, lambda k: (end - 1 - k, fine.nx - 1 - k))

    arrive(fine_halo, (1,))
    fine_part(0, edge, lambda k: (k + 1, edge + 1 + k))

    pool(lambda x, y: res_out[x, pl.ds(y, mid.n, stride=2), :], writer(sm, mid.margin, mid.n),
         mid.n, fine.stride)
    mid_halo = halo(((sm, mid, mid.margin),), FAR_FIRST)
    arrive(side_halo)
    setup(mid, at(km, mid.ny), at(am, mid.ny), wm)
    setup(coarse, at(kc, coarse.ny), at(ac, coarse.ny), wc)
    arrive(mid_halo)
    start_iterate(mid, of(sm), wm[4], um[0])

    def mid_finish(x, new, total, c, inv):
        midi[x] = total
        midr[x] = jnp.where(inv > 0.0, new, 0.0)

    sweeps(mid, of(sm), wm, rm, um, mid_finish)

    pool(lambda x, y: midr[x, pl.ds(y, coarse.n, stride=2), :],
         writer(sc, coarse.margin, coarse.n), coarse.n, mid.stride)
    coarse_halo = halo(((sc, coarse, coarse.margin),), FAR_FIRST)

    def pick(value, stride):
        cells = LANES // stride
        chosen = (lax.broadcasted_iota(jnp.int32, (LANES, cells), 0)
                  == stride * lax.broadcasted_iota(jnp.int32, (LANES, cells), 1)).astype(F32)
        return jnp.dot(value, chosen, preferred_element_type=F32, precision=lax.Precision.HIGHEST)

    mid_out[...] = pick(midi[...].reshape(mid.n * mid.n, LANES), mid.stride).reshape(mid_out.shape)
    arrive(coarse_halo)
    start_iterate(coarse, of(sc), wc[4], uc[0])
    a, b = coarse.steps[-1]

    def coarse_finish(x, new, total, c, inv):
        coai[x] = total + (a * c + b * (inv * new))

    sweeps(coarse, of(sc), wc, rc, uc, coarse_finish)
    coarse_out[...] = pick(coai[...].reshape(coarse.n * coarse.n, LANES),
                           coarse.stride).reshape(coarse_out.shape)

    for dx, dg in DIRS:
        @pl.when(target(dx, dg))
        def _(dx=dx, dg=dg):
            for group in groups:
                for copy in group[dx, dg]:
                    copy.wait_send()


def step(source, conductivity, absorption, brick_mask):
    n = source.shape[0]
    fine = Level(n, DEGREE, n + 2 * DEGREE, 1, STEP_SCALE, DEGREE, SMOOTH_LOW)
    mid = Level(n // 2, DEGREE, n // 2 + 2 * DEGREE, 2, STEP_SCALE / 4.0, DEGREE, SMOOTH_LOW)
    coarse = Level(n // 4, COARSE_DEGREE - 1, 24, 4, STEP_SCALE / 16.0, COARSE_DEGREE, COARSE_LOW)
    levels = (fine, mid, coarse)

    def kernel(*refs):
        body_kernel(levels, *refs)

    fields = []
    for level in levels:
        fields += [pltpu.VMEM(level.coefficient_shape(), F32), pltpu.VMEM(level.source_shape(), F32),
                   pltpu.VMEM(level.source_shape(), F32)]
    copies = 9 * len(DIRS)
    scratch = fields + [
        pltpu.VMEM((32, LANES), F32),
        pltpu.VMEM((mid.n, mid.n, LANES), F32),
        pltpu.VMEM((mid.n, mid.n, LANES), F32),
        pltpu.VMEM((coarse.n, coarse.n, LANES), F32),
    ]
    scratch += [[pltpu.VMEM(level.work_shape(), F32)] * 5 for level in levels]
    scratch += [pltpu.VMEM(level.work_shape(), F32) for level in levels]
    scratch += [[pltpu.VMEM(level.work_shape(), F32)] * count
                for level, count in zip(levels, (DEGREE, DEGREE, COARSE_DEGREE - 1))]
    scratch += [pltpu.SemaphoreType.DMA((3,)), pltpu.SemaphoreType.DMA((copies,)),
                pltpu.SemaphoreType.DMA((copies,))]
    vmem = pl.BlockSpec(memory_space=pltpu.VMEM)
    anywhere = pl.BlockSpec(memory_space=pl.ANY)
    shapes = ((n, n, LANES), (n, n, LANES), (mid.n, mid.n, LANES // 2), (coarse.n, coarse.n, LANES // 4))
    results = pl.pallas_call(
        kernel,
        out_shape=tuple(pltpu.VMEM(shape, F32) for shape in shapes),
        in_specs=[anywhere, anywhere, anywhere, vmem],
        out_specs=(vmem, vmem, vmem, vmem),
        scratch_shapes=scratch,
        compiler_params=pltpu.CompilerParams(collective_id=0, has_side_effects=True,
                                             vmem_limit_bytes=56 * 1024 * 1024),
    )(source, conductivity, absorption, brick_mask)

    def deliver(*refs):
        copies = [pltpu.make_async_copy(refs[i], refs[4 + i], refs[8].at[i]) for i in range(4)]
        for copy in copies:
            copy.start()
        for copy in copies:
            copy.wait()

    return pl.pallas_call(
        deliver,
        out_shape=tuple(jax.ShapeDtypeStruct(shape, F32) for shape in shapes),
        in_specs=[vmem] * 4,
        out_specs=(anywhere,) * 4,
        scratch_shapes=[pltpu.SemaphoreType.DMA((4,))],
    )(*(pltpu.with_memory_space_constraint(r, pltpu.VMEM) for r in results))


def solution(mesh):
    spec = P("dom", "grp", None)
    return jax.shard_map(step, mesh=mesh, in_specs=(spec,) * 4, out_specs=(spec,) * 4, check_vma=False)
```

```python
import jax
import jax.numpy as jnp
from jax import lax
from jax.experimental import pallas as pl
from jax.experimental.pallas import tpu as pltpu
from jax.sharding import PartitionSpec as P

DEGREE = 4
COARSE_DEGREE = 6
STEP_SCALE = 4.0
SMOOTH_LOW = 0.3
SMOOTH_HIGH = 2.0
COARSE_LOW = 0.05
LANES = 128
MESH = pl.DeviceIdType.MESH
DIRS = ((-1, 0), (1, 0), (0, 1), (0, -1), (-1, 1), (-1, -1), (1, 1), (1, -1))
BLOCK = 14
FAR_FIRST = ((1, 1), (1, -1), (-1, 1), (-1, -1), (1, 0), (-1, 0), (0, 1), (0, -1))
F32 = jnp.float32


def recurrence(degree, lowest, highest):
    middle = (highest + lowest) / 2.0
    spread = (highest - lowest) / 2.0
    relative = middle / spread
    factor = 1.0 / relative
    steps = []
    for _ in range(degree - 1):
        following = 1.0 / (2.0 * relative - factor)
        steps.append((following * factor, 2.0 * following / spread))
        factor = following
    return 1.0 / middle, tuple(steps)


class Level:
    def __init__(self, n, margin, rows, stride, scale, degree, lowest):
        self.n, self.margin, self.stride, self.scale = n, margin, stride, scale
        self.nx = n + 2 * margin
        self.y0 = 8 - margin
        self.ny = rows
        self.yb = 8 * ((self.y0 + rows + 1 + 7) // 8)
        self.first, self.steps = recurrence(degree, lowest, SMOOTH_HIGH)
        self.block = BLOCK if rows > 24 else 24

    def coefficient_shape(self):
        return (self.n + 2 * self.margin + 2, self.yb, LANES)

    def source_shape(self):
        return (self.nx, self.yb, LANES)

    def work_shape(self):
        return (self.nx, self.ny + 16, LANES)


def span(sign, n, margin):
    if sign == 0:
        return 0, n
    return (n - margin, margin) if sign > 0 else (0, margin)


def landing(sign, n, margin, offset):
    if sign == 0:
        return offset
    return offset - margin if sign > 0 else offset + n


def lane_index():
    return lax.broadcasted_iota(jnp.int32, (1, LANES), 1)


def blocks(low, high, body, most=BLOCK):
    steps, rest = divmod(high - low, most)

    def turn(s, carry):
        body(low + s * most, most)
        return carry

    if steps == 1:
        body(low, most)
    elif steps:
        lax.fori_loop(0, steps, turn, 0)
    if rest:
        body(high - rest, rest)


def pool(read, write, count, stride):
    even = lax.rem(lane_index() // stride, 2) == 0

    def body(first, rows):
        for i in range(rows):
            x = 2 * (first + i)
            p = (read(x, 0) + read(x, 1)) + (read(x + 1, 0) + read(x + 1, 1))
            other = jnp.where(even, pltpu.roll(p, LANES - stride, 1), pltpu.roll(p, stride, 1))
            write(first + i, (p + other) * 0.125)

    blocks(0, count, body)


def setup(level, kappa, absorb, work, source=None, u0=None, span_x=None):
    wx, wy, wz, diag, inv = work
    half = level.scale * 0.5
    up = lane_index() < LANES - level.stride
    down = lane_index() >= level.stride
    y0, ny = level.y0, level.ny

    def flag(k):
        return jnp.where(k > 0.0, 1.0, 0.0)

    def body(first, rows):
        ks = [kappa(first + x, y0) for x in range(rows + 2)]
        flags = [flag(k) for k in ks]
        for r in range(rows):
            i = first + r
            k, xp, xm = ks[r + 1], ks[r + 2], ks[r]
            yp, ym = kappa(i + 1, y0 + 1), kappa(i + 1, y0 - 1)
            zp = jnp.where(up, pltpu.roll(k, LANES - level.stride, 1), 0.0)
            zm = jnp.where(down, pltpu.roll(k, level.stride, 1), 0.0)
            total = (xp + xm) + (yp + ym) + (zp + zm)
            count = (flags[r + 2] + flags[r]) + (flag(yp) + flag(ym)) + (flag(zp) + flag(zm))
            d = (1.0 + half * (k * count + total)) + level.scale * absorb(i, y0) * (6.0 - count)
            at = pl.ds(8, ny)
            wx[i, at, :] = half * (k + xp)
            wy[i, at, :] = half * (k + yp)
            wz[i, at, :] = jnp.where(up, half * (k + zp), 0.0)
            diag[i, at, :] = d
            v = flags[r + 1] / d
            inv[i, at, :] = v
            if u0 is not None:
                u0[i, at, :] = (v * source(i, y0, ny)) * level.first

    blocks(*(span_x or (0, level.nx)), body, level.block)


def start_iterate(level, source, inv, u0):
    at = pl.ds(8, level.ny)

    def body(first, rows):
        for i in range(rows):
            u0[first + i, at, :] = (inv[first + i, at, :] * source(first + i, level.y0, level.ny)) * level.first

    blocks(0, level.nx, body, level.block)


def residual_rows(level, work, u, old, first, rows, start, size):
    wx, wy, wz, diag, inv = work
    at, above, below = pl.ds(start, size), pl.ds(start + 1, size), pl.ds(start - 1, size)
    us = [u[first + x - 1, at, :] for x in range(rows + 2)]
    ws = [wx[first + x - 1, at, :] for x in range(rows + 1)]
    out = []
    for r in range(rows):
        i, c = first + r, us[r + 1]
        t = ws[r + 1] * us[r + 2] + ws[r] * us[r]
        t = t + (wy[i, at, :] * u[i, above, :] + wy[i, below, :] * u[i, below, :])
        z = wz[i, at, :]
        t = t + (z * pltpu.roll(c, LANES - level.stride, 1) + pltpu.roll(z * c, level.stride, 1))
        out.append(((old(i) - diag[i, at, :] * c) + t, c))
    return out


def sweeps(level, source, work, r, us, finish, span_of=None):
    inv = work[4]
    last = len(us) - 1
    m, n = level.margin, level.n
    at = pl.ds(8, level.ny)
    span_of = span_of or (lambda k: (k + 1, level.nx - 1 - k))
    for k in range(last):
        a, b = level.steps[k]

        def body(first, rows, k=k, a=a, b=b):
            def old(i):
                return source(i, level.y0, level.ny) if k == 0 else r[i, at, :]

            for x, (new, c) in enumerate(
                    residual_rows(level, work, us[k], old, first, rows, 8, level.ny)):
                r[first + x, at, :] = new
                us[k + 1][first + x, at, :] = a * c + b * (inv[first + x, at, :] * new)

        blocks(*span_of(k), body, level.block)

    own = pl.ds(8 + m, n)

    def body(first, rows):
        for x, (new, c) in enumerate(
                residual_rows(level, work, us[last], lambda i: r[i, own, :], first, rows, 8 + m, n)):
            total = us[0][first + x, own, :]
            for u in us[1:-1]:
                total = total + u[first + x, own, :]
            finish(first + x - m, new, total + c, c, inv[first + x, own, :])

    blocks(*span_of(last), body, level.block)


def body_kernel(levels, s_in, k_in, a_in, b_in, it_out, res_out, mid_out, coarse_out,
                kf, sf, af, pm, sm, pc, sc, bm, fm, midr, midi, coai,
                wf, wm, wc, rf, rm, rc, uf, um, uc, local, send, recv, beyond):
    fine, mid, coarse = levels
    d, g = lax.axis_index("dom"), lax.axis_index("grp")
    nd, ng = lax.axis_size("dom"), lax.axis_size("grp")
    low_x, high_x = d > 0, d < nd - 1
    low_y, high_y = g > 0, g < ng - 1

    def both(p, q):
        return q if p is None else p if q is None else jnp.logical_and(p, q)

    def target(dx, dg):
        return both({0: None, 1: high_x, -1: low_x}[dx], {0: None, 1: high_y, -1: low_y}[dg])

    def neighbour(dx, dg):
        return (lax.rem(d + (nd + dx), nd), lax.rem(g + (ng + dg), ng))

    barrier = pltpu.get_barrier_semaphore()
    for dx, dg in DIRS[:4]:
        @pl.when(target(dx, dg))
        def _(dx=dx, dg=dg):
            pl.semaphore_signal(barrier, inc=1, device_id=neighbour(dx, dg), device_id_type=MESH)

    loads = []
    for slot, (operand, buffer, off) in enumerate(
            ((k_in, kf, fine.margin + 1), (a_in, af, fine.margin), (s_in, sf, fine.margin))):
        copy = pltpu.make_async_copy(operand, buffer.at[pl.ds(off, fine.n), pl.ds(8, fine.n), :],
                                     local.at[slot])
        copy.start()
        loads.append(copy)
    bricks = pltpu.make_async_copy(b_in, bm, local.at[3])
    bricks.start()

    fields = ((kf, fine, 1), (af, fine, 0), (sf, fine, 0), (pm, mid, 1), (sm, mid, 0),
              (pc, coarse, 1), (sc, coarse, 0))
    for ref, level, extra in fields:
        w = level.margin + extra
        rows, cells = level.n + 2 * w, level.n
        for missing, x0 in ((d == 0, 0), (d == nd - 1, w + cells)):
            @pl.when(missing)
            def _(ref=ref, level=level, w=w, x0=x0):
                for x in range(w):
                    ref[x0 + x] = jnp.zeros((level.yb, LANES), F32)
        for missing, y0 in ((g == 0, 0), (g == ng - 1, 8 + cells)):
            @pl.when(missing)
            def _(ref=ref, rows=rows, y0=y0):
                def clear(x, carry):
                    ref[x, pl.ds(y0, 8), :] = jnp.zeros((8, LANES), F32)
                    return carry
                lax.fori_loop(0, rows, clear, 0)

    count_x = low_x.astype(jnp.int32) + high_x.astype(jnp.int32) + 1
    count_y = low_y.astype(jnp.int32) + high_y.astype(jnp.int32) + 1

    pl.semaphore_wait(barrier, count_x + count_y - 2)
    for dg in (1, -1):
        @pl.when(target(0, dg))
        def _(dg=dg):
            pl.semaphore_signal(beyond, inc=1, device_id=neighbour(0, dg), device_id_type=MESH)

    used = [0]
    groups = []

    def halo(parts, order, before_corners=None):
        group = {}
        for dx, dg in order:
            if before_corners is not None and (dx, dg) == DIRS[4]:
                before_corners()
            copies = []
            for ref, level, width, operand in parts:
                n = level.n
                deep = width - 1 if dx and dg else width
                sx, cx = span(dx, n, deep)
                sy, cy = span(dg, n, deep)
                if operand is None:
                    src = ref.at[pl.ds(width + sx, cx), pl.ds(8 + sy, cy), :]
                else:
                    src = operand.at[pl.ds(sx, cx), pl.ds(sy, cy), :]
                slot = used[0]
                used[0] += 1
                copies.append(pltpu.make_async_remote_copy(
                    src_ref=src,
                    dst_ref=ref.at[pl.ds(landing(dx, n, deep, width), cx),
                                   pl.ds(landing(dg, n, deep, 8), cy), :],
                    send_sem=send.at[slot], recv_sem=recv.at[slot],
                    device_id=neighbour(dx, dg), device_id_type=MESH))

            @pl.when(target(dx, dg))
            def _(copies=copies):
                for copy in copies:
                    copy.start()

            group[dx, dg] = copies
        groups.append(group)
        return group

    def arrive(some, signs=(-1, 0, 1)):
        for dx, dg in DIRS:
            if dx not in signs:
                continue

            @pl.when(target(-dx, -dg))
            def _(dx=dx, dg=dg):
                for group in some:
                    for copy in group[dx, dg]:
                        copy.wait_recv()

    plain_halo = halo(((sf, fine, fine.margin, s_in), (af, fine, fine.margin, a_in)), DIRS,
                      lambda: pl.semaphore_wait(beyond, count_y - 1))
    lanes_of = (lax.broadcasted_iota(jnp.int32, (16, LANES), 1) // 8
                == lax.broadcasted_iota(jnp.int32, (16, LANES), 0)).astype(F32)
    bricks.wait()
    for bx in range(4):
        fm[pl.ds(8 * bx, 4), :] = jnp.dot(bm[bx].astype(F32), lanes_of, preferred_element_type=F32)

    loads[0].wait()
    kx = fine.margin + 1

    def mask_own(s, carry):
        for t in range(4):
            flag = jnp.broadcast_to(fm[pl.ds(8 * (s // 2) + t, 1), :], (8, LANES))
            for x in range(4):
                at = (kx + 4 * s + x, pl.ds(8 + 8 * t, 8), slice(None))
                kf[at] = kf[at] * flag
        return carry

    lax.fori_loop(0, fine.n // 4, mask_own, 0)
    fine_halo = halo(((kf, fine, kx, None),), DIRS)
    loads[1].wait()
    loads[2].wait()

    mx, cx = mid.margin + 1, coarse.margin + 1
    lane = lane_index()

    def quad(ref, x, y0, count):
        lower, upper = pl.ds(y0, count, stride=2), pl.ds(y0 + 1, count, stride=2)
        return (ref[x, lower, :] + ref[x, upper, :]) + (ref[x + 1, lower, :] + ref[x + 1, upper, :])

    def pack_mid(first, rows):
        for r in range(rows):
            x = first + r
            k = quad(kf, kx + 2 * x, 8, mid.n)
            a = quad(af, fine.margin + 2 * x, 8, mid.n)
            pm[mx + x, pl.ds(8, mid.n), :] = 0.125 * jnp.where(
                lane % 2 == 0, k + pltpu.roll(k, LANES - 1, 1), a + pltpu.roll(a, 1, 1))

    blocks(0, mid.n, pack_mid, 8)

    def pack_coarse(first, rows):
        for r in range(rows):
            x = first + r
            p = quad(pm, mx + 2 * x, 8, coarse.n)
            q = p + jnp.where(lane % 4 < 2, pltpu.roll(p, LANES - 2, 1), pltpu.roll(p, 2, 1))
            inner = jnp.where(lane % 4 == 1, pltpu.roll(q, 1, 1), pltpu.roll(q, LANES - 1, 1))
            outer = jnp.logical_or(lane % 4 == 0, lane % 4 == 3)
            pc[cx + x, pl.ds(8, coarse.n), :] = 0.125 * jnp.where(outer, q, inner)

    blocks(0, coarse.n, pack_coarse, 8)
    side_halo = halo(((pm, mid, mx, None), (pc, coarse, cx, None)), DIRS)

    def unpack(ref, level):
        half = level.stride // 2
        first = (lane // half) % 2 == 0

        def kappa(x, y):
            p = ref[x, pl.ds(y, level.ny), :]
            return jnp.where(first, p, pltpu.roll(p, half, 1))

        def absorb(x, y):
            p = ref[x + 1, pl.ds(y, level.ny), :]
            return jnp.where(first, pltpu.roll(p, LANES - half, 1), p)

        return kappa, absorb

    def writer(ref, x0, count):
        def write(x, value):
            ref[x + x0, pl.ds(8, count), :] = value
        return write

    def at(ref, size):
        return lambda x, y: ref[x, pl.ds(y, size), :]

    def of(ref):
        return lambda x, y, size: ref[x, pl.ds(y, size), :]

    def fine_finish(x, new, total, c, inv):
        it_out[x] = total
        res_out[x] = jnp.where(inv > 0.0, new, 0.0)

    def fine_part(low, high, span_of):
        setup(fine, at(kf, fine.ny), at(af, fine.ny), wf, of(sf), uf[0], (low, high))
        sweeps(fine, of(sf), wf, rf, uf, fine_finish, span_of)

    edge, end = fine.margin + 1, fine.nx - fine.margin - 1
    fine_groups = (plain_halo, fine_halo)
    arrive(fine_groups, (0,))
    fine_part(edge, end, lambda k: (edge + 1 + k, end - 1 - k))
    arrive(fine_groups, (-1,))
    fine_part(end, fine.nx, lambda k: (end - 1 - k, fine.nx - 1 - k))

    arrive(fine_groups, (1,))
    fine_part(0, edge, lambda k: (k + 1, edge + 1 + k))

    pool(lambda x, y: res_out[x, pl.ds(y, mid.n, stride=2), :], writer(sm, mid.margin, mid.n),
         mid.n, fine.stride)
    mid_halo = halo(((sm, mid, mid.margin, None),), FAR_FIRST)
    arrive((side_halo,))
    setup(mid, *unpack(pm, mid), wm)
    setup(coarse, *unpack(pc, coarse), wc)
    arrive((mid_halo,))
    start_iterate(mid, of(sm), wm[4], um[0])

    def mid_finish(x, new, total, c, inv):
        midi[x] = total
        midr[x] = jnp.where(inv > 0.0, new, 0.0)

    sweeps(mid, of(sm), wm, rm, um, mid_finish)

    pool(lambda x, y: midr[x, pl.ds(y, coarse.n, stride=2), :],
         writer(sc, coarse.margin, coarse.n), coarse.n, mid.stride)
    coarse_halo = halo(((sc, coarse, coarse.margin, None),), FAR_FIRST)

    def pick(value, stride):
        cells = LANES // stride
        chosen = (lax.broadcasted_iota(jnp.int32, (LANES, cells), 0)
                  == stride * lax.broadcasted_iota(jnp.int32, (LANES, cells), 1)).astype(F32)
        return jnp.dot(value, chosen, preferred_element_type=F32, precision=lax.Precision.HIGHEST)

    mid_out[...] = pick(midi[...].reshape(mid.n * mid.n, LANES), mid.stride).reshape(mid_out.shape)
    arrive((coarse_halo,))
    start_iterate(coarse, of(sc), wc[4], uc[0])
    a, b = coarse.steps[-1]

    def coarse_finish(x, new, total, c, inv):
        coai[x] = total + (a * c + b * (inv * new))

    sweeps(coarse, of(sc), wc, rc, uc, coarse_finish)
    coarse_out[...] = pick(coai[...].reshape(coarse.n * coarse.n, LANES),
                           coarse.stride).reshape(coarse_out.shape)

    for dx, dg in DIRS:
        @pl.when(target(dx, dg))
        def _(dx=dx, dg=dg):
            for group in groups:
                for copy in group[dx, dg]:
                    copy.wait_send()


def step(source, conductivity, absorption, brick_mask):
    n = source.shape[0]
    fine = Level(n, DEGREE, n + 2 * DEGREE, 1, STEP_SCALE, DEGREE, SMOOTH_LOW)
    mid = Level(n // 2, DEGREE, n // 2 + 2 * DEGREE, 2, STEP_SCALE / 4.0, DEGREE, SMOOTH_LOW)
    coarse = Level(n // 4, COARSE_DEGREE - 1, 24, 4, STEP_SCALE / 16.0, COARSE_DEGREE, COARSE_LOW)
    levels = (fine, mid, coarse)

    def kernel(*refs):
        body_kernel(levels, *refs)

    fields = [pltpu.VMEM(fine.coefficient_shape(), F32)] + [pltpu.VMEM(fine.source_shape(), F32)] * 2
    for level in (mid, coarse):
        fields += [pltpu.VMEM(level.coefficient_shape(), F32), pltpu.VMEM(level.source_shape(), F32)]
    copies = 7 * len(DIRS)
    scratch = fields + [
        pltpu.VMEM(brick_mask.shape, jnp.int32),
        pltpu.VMEM((32, LANES), F32),
        pltpu.VMEM((mid.n, mid.n, LANES), F32),
        pltpu.VMEM((mid.n, mid.n, LANES), F32),
        pltpu.VMEM((coarse.n, coarse.n, LANES), F32),
    ]
    scratch += [[pltpu.VMEM(level.work_shape(), F32)] * 5 for level in levels]
    scratch += [pltpu.VMEM(level.work_shape(), F32) for level in levels]
    scratch += [[pltpu.VMEM(level.work_shape(), F32)] * count
                for level, count in zip(levels, (DEGREE, DEGREE, COARSE_DEGREE - 1))]
    scratch += [pltpu.SemaphoreType.DMA((4,)), pltpu.SemaphoreType.DMA((copies,)),
                pltpu.SemaphoreType.DMA((copies,)), pltpu.SemaphoreType.REGULAR]
    vmem = pl.BlockSpec(memory_space=pltpu.VMEM)
    anywhere = pl.BlockSpec(memory_space=pl.ANY)
    shapes = ((n, n, LANES), (n, n, LANES), (mid.n, mid.n, LANES // 2), (coarse.n, coarse.n, LANES // 4))
    results = pl.pallas_call(
        kernel,
        out_shape=tuple(pltpu.VMEM(shape, F32) for shape in shapes),
        in_specs=[anywhere] * 4,
        out_specs=(vmem, vmem, vmem, vmem),
        scratch_shapes=scratch,
        compiler_params=pltpu.CompilerParams(collective_id=0, has_side_effects=True,
                                             vmem_limit_bytes=56 * 1024 * 1024),
    )(source, conductivity, absorption, brick_mask)

    def deliver(*refs):
        copies = [pltpu.make_async_copy(refs[i], refs[4 + i], refs[8].at[i]) for i in range(4)]
        for copy in copies:
            copy.start()
        for copy in copies:
            copy.wait()

    return pl.pallas_call(
        deliver,
        out_shape=tuple(jax.ShapeDtypeStruct(shape, F32) for shape in shapes),
        in_specs=[vmem] * 4,
        out_specs=(anywhere,) * 4,
        scratch_shapes=[pltpu.SemaphoreType.DMA((4,))],
    )(*(pltpu.with_memory_space_constraint(r, pltpu.VMEM) for r in results))


def solution(mesh):
    spec = P("dom", "grp", None)
    return jax.shard_map(step, mesh=mesh, in_specs=(spec,) * 4, out_specs=(spec,) * 4, check_vma=False)
```

```python
import jax
import jax.numpy as jnp
from jax import lax
from jax.experimental import pallas as pl
from jax.experimental.pallas import tpu as pltpu
from jax.sharding import PartitionSpec as P

DEGREE = 4
COARSE_DEGREE = 6
STEP_SCALE = 4.0
SMOOTH_LOW = 0.3
SMOOTH_HIGH = 2.0
COARSE_LOW = 0.05
LANES = 128
MESH = pl.DeviceIdType.MESH
DIRS = ((-1, 0), (1, 0), (0, 1), (0, -1), (-1, 1), (-1, -1), (1, 1), (1, -1))
BLOCK = 14
FAR_FIRST = ((1, 1), (1, -1), (-1, 1), (-1, -1), (1, 0), (-1, 0), (0, 1), (0, -1))
F32 = jnp.float32


def recurrence(degree, lowest, highest):
    middle = (highest + lowest) / 2.0
    spread = (highest - lowest) / 2.0
    relative = middle / spread
    factor = 1.0 / relative
    steps = []
    for _ in range(degree - 1):
        following = 1.0 / (2.0 * relative - factor)
        steps.append((following * factor, 2.0 * following / spread))
        factor = following
    return 1.0 / middle, tuple(steps)


class Level:
    def __init__(self, n, margin, rows, stride, scale, degree, lowest):
        self.n, self.margin, self.stride, self.scale = n, margin, stride, scale
        self.nx = n + 2 * margin
        self.y0 = 8 - margin
        self.ny = rows
        self.yb = 8 * ((self.y0 + rows + 1 + 7) // 8)
        self.first, self.steps = recurrence(degree, lowest, SMOOTH_HIGH)
        self.block = BLOCK if rows > 24 else 24

    def coefficient_shape(self):
        return (self.n + 2 * self.margin + 2, self.yb, LANES)

    def source_shape(self):
        return (self.nx, self.yb, LANES)

    def work_shape(self):
        return (self.nx, self.ny + 16, LANES)


def span(sign, n, margin):
    if sign == 0:
        return 0, n
    return (n - margin, margin) if sign > 0 else (0, margin)


def landing(sign, n, margin, offset):
    if sign == 0:
        return offset
    return offset - margin if sign > 0 else offset + n


def lane_index():
    return lax.broadcasted_iota(jnp.int32, (1, LANES), 1)


def blocks(low, high, body, most=BLOCK):
    steps, rest = divmod(high - low, most)

    def turn(s, carry):
        body(low + s * most, most)
        return carry

    if steps == 1:
        body(low, most)
    elif steps:
        lax.fori_loop(0, steps, turn, 0)
    if rest:
        body(high - rest, rest)


def pool(read, write, count, stride):
    even = lax.rem(lane_index() // stride, 2) == 0

    def body(first, rows):
        for i in range(rows):
            x = 2 * (first + i)
            p = (read(x, 0) + read(x, 1)) + (read(x + 1, 0) + read(x + 1, 1))
            other = jnp.where(even, pltpu.roll(p, LANES - stride, 1), pltpu.roll(p, stride, 1))
            write(first + i, (p + other) * 0.125)

    blocks(0, count, body, count)


def setup(level, kappa, absorb, work, source=None, u0=None, span_x=None, span_y=None):
    wx, wy, wz, diag, inv = work
    half = level.scale * 0.5
    up = lane_index() < LANES - level.stride
    down = lane_index() >= level.stride
    skip, ny = span_y or (0, level.ny)
    y0 = level.y0 + skip

    def flag(k):
        return jnp.where(k > 0.0, 1.0, 0.0)

    def body(first, rows):
        ks = [kappa(first + x, y0) for x in range(rows + 2)]
        flags = [flag(k) for k in ks]
        for r in range(rows):
            i = first + r
            k, xp, xm = ks[r + 1], ks[r + 2], ks[r]
            yp, ym = kappa(i + 1, y0 + 1), kappa(i + 1, y0 - 1)
            zp = jnp.where(up, pltpu.roll(k, LANES - level.stride, 1), 0.0)
            zm = jnp.where(down, pltpu.roll(k, level.stride, 1), 0.0)
            total = (xp + xm) + (yp + ym) + (zp + zm)
            count = (flags[r + 2] + flags[r]) + (flag(yp) + flag(ym)) + (flag(zp) + flag(zm))
            d = (1.0 + half * (k * count + total)) + level.scale * absorb(i, y0) * (6.0 - count)
            at = pl.ds(8 + skip, ny)
            wx[i, at, :] = half * (k + xp)
            wy[i, at, :] = half * (k + yp)
            wz[i, at, :] = jnp.where(up, half * (k + zp), 0.0)
            diag[i, at, :] = d
            v = flags[r + 1] / d
            inv[i, at, :] = v
            if u0 is not None:
                u0[i, at, :] = (v * source(i, y0, ny)) * level.first

    blocks(*(span_x or (0, level.nx)), body, level.block)


def start_iterate(level, source, inv, u0):
    at = pl.ds(8, level.ny)

    def body(first, rows):
        for i in range(rows):
            u0[first + i, at, :] = (inv[first + i, at, :] * source(first + i, level.y0, level.ny)) * level.first

    blocks(0, level.nx, body, level.block)


def residual_rows(level, work, u, old, first, rows, start, size):
    wx, wy, wz, diag, inv = work
    at, above, below = pl.ds(start, size), pl.ds(start + 1, size), pl.ds(start - 1, size)
    us = [u[first + x - 1, at, :] for x in range(rows + 2)]
    ws = [wx[first + x - 1, at, :] for x in range(rows + 1)]
    out = []
    for r in range(rows):
        i, c = first + r, us[r + 1]
        t = ws[r + 1] * us[r + 2] + ws[r] * us[r]
        t = t + (wy[i, at, :] * u[i, above, :] + wy[i, below, :] * u[i, below, :])
        z = wz[i, at, :]
        t = t + (z * pltpu.roll(c, LANES - level.stride, 1) + pltpu.roll(z * c, level.stride, 1))
        out.append(((old(i) - diag[i, at, :] * c) + t, c))
    return out


def sweeps(level, source, work, r, us, finish, span_of=None):
    inv = work[4]
    last = len(us) - 1
    m, n = level.margin, level.n
    at = pl.ds(8, level.ny)
    span_of = span_of or (lambda k: (k + 1, level.nx - 1 - k))
    for k in range(last):
        a, b = level.steps[k]

        def body(first, rows, k=k, a=a, b=b):
            def old(i):
                return source(i, level.y0, level.ny) if k == 0 else r[i, at, :]

            for x, (new, c) in enumerate(
                    residual_rows(level, work, us[k], old, first, rows, 8, level.ny)):
                r[first + x, at, :] = new
                us[k + 1][first + x, at, :] = a * c + b * (inv[first + x, at, :] * new)

        blocks(*span_of(k), body, level.block)

    own = pl.ds(8 + m, n)

    def body(first, rows):
        for x, (new, c) in enumerate(
                residual_rows(level, work, us[last], lambda i: r[i, own, :], first, rows, 8 + m, n)):
            total = us[0][first + x, own, :]
            for u in us[1:-1]:
                total = total + u[first + x, own, :]
            finish(first + x - m, new, total + c, c, inv[first + x, own, :])

    blocks(*span_of(last), body, level.block)


def body_kernel(levels, s_in, k_in, a_in, b_in, it_out, res_out, mid_out, coarse_out,
                kf, sf, af, pm, sm, pc, sc, bm, fm, midr, midi, coai,
                wf, wm, wc, rf, rm, rc, uf, um, uc, local, send, recv, beyond):
    fine, mid, coarse = levels
    d, g = lax.axis_index("dom"), lax.axis_index("grp")
    nd, ng = lax.axis_size("dom"), lax.axis_size("grp")
    low_x, high_x = d > 0, d < nd - 1
    low_y, high_y = g > 0, g < ng - 1

    def both(p, q):
        return q if p is None else p if q is None else jnp.logical_and(p, q)

    def target(dx, dg):
        return both({0: None, 1: high_x, -1: low_x}[dx], {0: None, 1: high_y, -1: low_y}[dg])

    def neighbour(dx, dg):
        return (lax.rem(d + (nd + dx), nd), lax.rem(g + (ng + dg), ng))

    barrier = pltpu.get_barrier_semaphore()
    for dx, dg in DIRS[:4]:
        @pl.when(target(dx, dg))
        def _(dx=dx, dg=dg):
            pl.semaphore_signal(barrier, inc=1, device_id=neighbour(dx, dg), device_id_type=MESH)

    loads = []
    for slot, (operand, buffer, off) in enumerate(
            ((k_in, kf, fine.margin + 1), (a_in, af, fine.margin), (s_in, sf, fine.margin))):
        copy = pltpu.make_async_copy(operand, buffer.at[pl.ds(off, fine.n), pl.ds(8, fine.n), :],
                                     local.at[slot])
        copy.start()
        loads.append(copy)
    bricks = pltpu.make_async_copy(b_in, bm, local.at[3])
    bricks.start()

    fields = ((kf, fine, 1, False), (af, fine, 0, False), (sf, fine, 0, False), (pm, mid, 1, False),
              (sm, mid, 0, True), (pc, coarse, 1, False), (sc, coarse, 0, True))
    for ref, level, extra, paired in fields:
        w, deep, cells = level.margin + extra, level.n, level.n
        if paired:
            w, deep = (w + 1) // 2, cells // 2
        rows = deep + 2 * w
        for missing, x0 in ((d == 0, 0), (d == nd - 1, w + deep)):
            @pl.when(missing)
            def _(ref=ref, level=level, w=w, x0=x0):
                for x in range(w):
                    ref[x0 + x] = jnp.zeros((level.yb, LANES), F32)
        for missing, y0 in ((g == 0, 0), (g == ng - 1, 8 + cells)):
            @pl.when(missing)
            def _(ref=ref, rows=rows, y0=y0):
                def clear(x, carry):
                    ref[x, pl.ds(y0, 8), :] = jnp.zeros((8, LANES), F32)
                    return carry
                lax.fori_loop(0, rows, clear, 0)

    count_x = low_x.astype(jnp.int32) + high_x.astype(jnp.int32) + 1
    count_y = low_y.astype(jnp.int32) + high_y.astype(jnp.int32) + 1

    pl.semaphore_wait(barrier, count_x + count_y - 2)
    for dg in (1, -1):
        @pl.when(target(0, dg))
        def _(dg=dg):
            pl.semaphore_signal(beyond, inc=1, device_id=neighbour(0, dg), device_id_type=MESH)

    used = [0]
    groups = []

    def halo(parts, order, before_corners=None):
        group = {}
        for dx, dg in order:
            if before_corners is not None and (dx, dg) == DIRS[4]:
                before_corners()
            copies = []
            for ref, level, width, operand, paired in parts:
                n = level.n
                deep = width - 1 if dx and dg else width
                rows, border, deep_x = n, width, deep
                if paired:
                    rows, border, deep_x = n // 2, (width + 1) // 2, (deep + 1) // 2
                sx, cx = span(dx, rows, deep_x)
                sy, cy = span(dg, n, deep)
                if operand is None:
                    src = ref.at[pl.ds(border + sx, cx), pl.ds(8 + sy, cy), :]
                else:
                    src = operand.at[pl.ds(sx, cx), pl.ds(sy, cy), :]
                slot = used[0]
                used[0] += 1
                copies.append(pltpu.make_async_remote_copy(
                    src_ref=src,
                    dst_ref=ref.at[pl.ds(landing(dx, rows, deep_x, border), cx),
                                   pl.ds(landing(dg, n, deep, 8), cy), :],
                    send_sem=send.at[slot], recv_sem=recv.at[slot],
                    device_id=neighbour(dx, dg), device_id_type=MESH))

            @pl.when(target(dx, dg))
            def _(copies=copies):
                for copy in copies:
                    copy.start()

            group[dx, dg] = copies
        groups.append(group)
        return group

    def arrive(some, signs=(-1, 0, 1)):
        for dx, dg in DIRS:
            if dx not in signs:
                continue

            @pl.when(target(-dx, -dg))
            def _(dx=dx, dg=dg):
                for group in some:
                    for copy in group[dx, dg]:
                        copy.wait_recv()

    plain_halo = halo(((sf, fine, fine.margin, s_in, False), (af, fine, fine.margin, a_in, False)), DIRS,
                      lambda: pl.semaphore_wait(beyond, count_y - 1))
    lanes_of = (lax.broadcasted_iota(jnp.int32, (16, LANES), 1) // 8
                == lax.broadcasted_iota(jnp.int32, (16, LANES), 0)).astype(F32)
    bricks.wait()
    for bx in range(4):
        fm[pl.ds(8 * bx, 4), :] = jnp.dot(bm[bx].astype(F32), lanes_of, preferred_element_type=F32)

    loads[0].wait()
    kx = fine.margin + 1

    def mask_own(s, carry):
        for t in range(4):
            flag = jnp.broadcast_to(fm[pl.ds(8 * (s // 2) + t, 1), :], (8, LANES))
            for x in range(4):
                at = (kx + 4 * s + x, pl.ds(8 + 8 * t, 8), slice(None))
                kf[at] = kf[at] * flag
        return carry

    lax.fori_loop(0, fine.n // 4, mask_own, 0)
    fine_halo = halo(((kf, fine, kx, None, False),), DIRS)
    loads[1].wait()
    loads[2].wait()

    mx, cx = mid.margin + 1, coarse.margin + 1
    lane = lane_index()

    def quad(ref, x, y0, count):
        lower, upper = pl.ds(y0, count, stride=2), pl.ds(y0 + 1, count, stride=2)
        return (ref[x, lower, :] + ref[x, upper, :]) + (ref[x + 1, lower, :] + ref[x + 1, upper, :])

    def pack_mid(first, rows):
        for r in range(rows):
            x = first + r
            k = quad(kf, kx + 2 * x, 8, mid.n)
            a = quad(af, fine.margin + 2 * x, 8, mid.n)
            pm[mx + x, pl.ds(8, mid.n), :] = 0.125 * jnp.where(
                lane % 2 == 0, k + pltpu.roll(k, LANES - 1, 1), a + pltpu.roll(a, 1, 1))

    blocks(0, mid.n, pack_mid, 8)

    def pack_coarse(first, rows):
        for r in range(rows):
            x = first + r
            p = quad(pm, mx + 2 * x, 8, coarse.n)
            q = p + jnp.where(lane % 4 < 2, pltpu.roll(p, LANES - 2, 1), pltpu.roll(p, 2, 1))
            inner = jnp.where(lane % 4 == 1, pltpu.roll(q, 1, 1), pltpu.roll(q, LANES - 1, 1))
            outer = jnp.logical_or(lane % 4 == 0, lane % 4 == 3)
            pc[cx + x, pl.ds(8, coarse.n), :] = 0.125 * jnp.where(outer, q, inner)

    blocks(0, coarse.n, pack_coarse, 8)
    side_halo = halo(((pm, mid, mx, None, False), (pc, coarse, cx, None, False)), DIRS)

    def unpack(ref, level):
        half = level.stride // 2
        first = (lane // half) % 2 == 0

        def kappa(x, y):
            p = ref[x, pl.ds(y, level.ny), :]
            return jnp.where(first, p, pltpu.roll(p, half, 1))

        def absorb(x, y):
            p = ref[x + 1, pl.ds(y, level.ny), :]
            return jnp.where(first, pltpu.roll(p, LANES - half, 1), p)

        return kappa, absorb

    def paired_rows(ref, level):
        half = level.stride // 2
        first = (lane // half) % 2 == 0
        border = (level.margin + 1) // 2
        held = []

        def write(x, value):
            held.append(value)
            if x % 2 == 1:
                odd, even = held.pop(), held.pop()
                ref[border + x // 2, pl.ds(8, level.n), :] = jnp.where(first, even, odd)

        def read(i, y, size):
            q = i + 2 * border - level.margin
            p = ref[q // 2, pl.ds(y, size), :]
            if q % 2 == 0:
                return jnp.where(first, p, pltpu.roll(p, half, 1))
            return jnp.where(first, pltpu.roll(p, LANES - half, 1), p)

        return write, read

    def at(ref, size):
        return lambda x, y: ref[x, pl.ds(y, size), :]

    def of(ref):
        return lambda x, y, size: ref[x, pl.ds(y, size), :]

    def fine_finish(x, new, total, c, inv):
        it_out[x] = total
        res_out[x] = jnp.where(inv > 0.0, new, 0.0)

    def fine_setup(low, high, skip, size):
        setup(fine, at(kf, size), at(af, size), wf, of(sf), uf[0], (low, high), (skip, size))

    def fine_part(low, high, span_of, ready=False):
        if not ready:
            fine_setup(low, high, 0, fine.ny)
        sweeps(fine, of(sf), wf, rf, uf, fine_finish, span_of)

    edge, end = fine.margin + 1, fine.nx - fine.margin - 1
    fine_groups = (plain_halo, fine_halo)
    fine_setup(edge, end, 8, fine.ny - 16)
    arrive(fine_groups, (0,))
    fine_setup(edge, end, 0, 8)
    fine_setup(edge, end, fine.ny - 8, 8)
    fine_part(edge, end, lambda k: (edge + 1 + k, end - 1 - k), ready=True)

    arrive(fine_groups, (-1,))
    fine_part(end, fine.nx, lambda k: (end - 1 - k, fine.nx - 1 - k))
    arrive(fine_groups, (1,))
    fine_part(0, edge, lambda k: (k + 1, edge + 1 + k))

    put, mid_source = paired_rows(sm, mid)
    pool(lambda x, y: res_out[x, pl.ds(y, mid.n, stride=2), :], put, mid.n, fine.stride)
    mid_halo = halo(((sm, mid, mid.margin, None, True),), FAR_FIRST)
    arrive((side_halo,))
    setup(mid, *unpack(pm, mid), wm)
    setup(coarse, *unpack(pc, coarse), wc)
    arrive((mid_halo,))
    start_iterate(mid, mid_source, wm[4], um[0])

    def mid_finish(x, new, total, c, inv):
        midi[x] = total
        midr[x] = jnp.where(inv > 0.0, new, 0.0)

    sweeps(mid, mid_source, wm, rm, um, mid_finish)

    put, coarse_source = paired_rows(sc, coarse)
    pool(lambda x, y: midr[x, pl.ds(y, coarse.n, stride=2), :], put, coarse.n, mid.stride)
    coarse_halo = halo(((sc, coarse, coarse.margin, None, True),), FAR_FIRST)

    def pick(value, stride):
        cells = LANES // stride
        chosen = (lax.broadcasted_iota(jnp.int32, (LANES, cells), 0)
                  == stride * lax.broadcasted_iota(jnp.int32, (LANES, cells), 1)).astype(F32)
        return jnp.dot(value, chosen, preferred_element_type=F32, precision=lax.Precision.HIGHEST)

    mid_out[...] = pick(midi[...].reshape(mid.n * mid.n, LANES), mid.stride).reshape(mid_out.shape)
    arrive((coarse_halo,))
    start_iterate(coarse, coarse_source, wc[4], uc[0])
    a, b = coarse.steps[-1]

    def coarse_finish(x, new, total, c, inv):
        coai[x] = total + (a * c + b * (inv * new))

    sweeps(coarse, coarse_source, wc, rc, uc, coarse_finish)
    coarse_out[...] = pick(coai[...].reshape(coarse.n * coarse.n, LANES),
                           coarse.stride).reshape(coarse_out.shape)

    for dx, dg in DIRS:
        @pl.when(target(dx, dg))
        def _(dx=dx, dg=dg):
            for group in groups:
                for copy in group[dx, dg]:
                    copy.wait_send()


def step(source, conductivity, absorption, brick_mask):
    n = source.shape[0]
    fine = Level(n, DEGREE, n + 2 * DEGREE, 1, STEP_SCALE, DEGREE, SMOOTH_LOW)
    mid = Level(n // 2, DEGREE, n // 2 + 2 * DEGREE, 2, STEP_SCALE / 4.0, DEGREE, SMOOTH_LOW)
    coarse = Level(n // 4, COARSE_DEGREE - 1, 24, 4, STEP_SCALE / 16.0, COARSE_DEGREE, COARSE_LOW)
    levels = (fine, mid, coarse)

    def kernel(*refs):
        body_kernel(levels, *refs)

    fields = [pltpu.VMEM(fine.coefficient_shape(), F32)] + [pltpu.VMEM(fine.source_shape(), F32)] * 2
    for level in (mid, coarse):
        pairs = level.n // 2 + 2 * ((level.margin + 1) // 2)
        fields += [pltpu.VMEM(level.coefficient_shape(), F32), pltpu.VMEM((pairs, level.yb, LANES), F32)]
    copies = 7 * len(DIRS)
    scratch = fields + [
        pltpu.VMEM(brick_mask.shape, jnp.int32),
        pltpu.VMEM((32, LANES), F32),
        pltpu.VMEM((mid.n, mid.n, LANES), F32),
        pltpu.VMEM((mid.n, mid.n, LANES), F32),
        pltpu.VMEM((coarse.n, coarse.n, LANES), F32),
    ]
    scratch += [[pltpu.VMEM(level.work_shape(), F32)] * 5 for level in levels]
    scratch += [pltpu.VMEM(level.work_shape(), F32) for level in levels]
    scratch += [[pltpu.VMEM(level.work_shape(), F32)] * count
                for level, count in zip(levels, (DEGREE, DEGREE, COARSE_DEGREE - 1))]
    scratch += [pltpu.SemaphoreType.DMA((4,)), pltpu.SemaphoreType.DMA((copies,)),
                pltpu.SemaphoreType.DMA((copies,)), pltpu.SemaphoreType.REGULAR]
    vmem = pl.BlockSpec(memory_space=pltpu.VMEM)
    anywhere = pl.BlockSpec(memory_space=pl.ANY)
    shapes = ((n, n, LANES), (n, n, LANES), (mid.n, mid.n, LANES // 2), (coarse.n, coarse.n, LANES // 4))
    results = pl.pallas_call(
        kernel,
        out_shape=tuple(pltpu.VMEM(shape, F32) for shape in shapes),
        in_specs=[anywhere] * 4,
        out_specs=(vmem, vmem, vmem, vmem),
        scratch_shapes=scratch,
        compiler_params=pltpu.CompilerParams(collective_id=0, has_side_effects=True,
                                             vmem_limit_bytes=56 * 1024 * 1024),
    )(source, conductivity, absorption, brick_mask)

    def deliver(*refs):
        copies = [pltpu.make_async_copy(refs[i], refs[4 + i], refs[8].at[i]) for i in range(4)]
        for copy in copies:
            copy.start()
        for copy in copies:
            copy.wait()

    return pl.pallas_call(
        deliver,
        out_shape=tuple(jax.ShapeDtypeStruct(shape, F32) for shape in shapes),
        in_specs=[vmem] * 4,
        out_specs=(anywhere,) * 4,
        scratch_shapes=[pltpu.SemaphoreType.DMA((4,))],
    )(*(pltpu.with_memory_space_constraint(r, pltpu.VMEM) for r in results))


def solution(mesh):
    spec = P("dom", "grp", None)
    return jax.shard_map(step, mesh=mesh, in_specs=(spec,) * 4, out_specs=(spec,) * 4, check_vma=False)
```
